512 devices in a mesh: ens: 32 (over z, y_lo, core), pen: 16 (over x, y_hi).
Axes of the slice: x: 4, y: 8 (y_hi: 4, y_lo: 2; y = y_hi * 2 + y_lo), z: 8, core: 2. Of those that a mesh axis runs over, the one named last changes fastest.
Arguments:
- state: float32 [2, 32, 4, 256, 512], P(None, 'ens', None, 'pen'), may hold values from -8 to 8, as said below
- accum: float32 [2, 32, 4, 256, 512], P(None, 'ens', None, 'pen'), may hold values from -8 to 8, as said below
- base_flow: float32 [6, 4, 256, 256], P(None, None, 'pen', 'ens'), may hold values from -6 to 6
Outputs:
- state_next: float32 [2, 32, 4, 256, 512], P(None, 'ens', None, 'pen')
- accum_next: float32 [2, 32, 4, 256, 512], P(None, 'ens', None, 'pen')
The draws below stay inside these ranges and needn't reach their ends.
Inputs may be any that keep to these rules, and one draw needn't show every extreme that they name: `state`: each field of each perturbation and level is the spectrum of a real field: the entry at ((256 - ky) mod 256, (256 - kx) mod 256) is the complex conjugate of the entry at (ky, kx). `accum`: each field of each perturbation and level is the spectrum of a real field: the entry at ((256 - ky) mod 256, (256 - kx) mod 256) is the complex conjugate of the entry at (ky, kx).
All inputs are finite; a program needn't handle non-finite values.
Results may differ from the reference program's by a relative error of at most 0.0003.
Values sent between devices are 32-bit elements; how exact they have to be, the bound alone decides.
A program may use at most 64 MiB of HBM per device.

```python
import math
import jax
import jax.numpy as jnp
from jax import lax

GRID = 256
LEVELS = 4
PERTS = 32


def reflect(values):
    return jnp.roll(jnp.flip(values, axis=(-1, -2)), 1, axis=(-1, -2))


def hermitian(key):
    full_shape = (2, PERTS, LEVELS, GRID, GRID)
    key_real, key_imag = jax.random.split(key)
    real_part = 1.4142 * jax.random.truncated_normal(key_real, -5.0, 5.0, full_shape, jnp.float32)
    imag_part = 1.4142 * jax.random.truncated_normal(key_imag, -5.0, 5.0, full_shape, jnp.float32)
    real_part = 0.5 * (real_part + reflect(real_part))
    imag_part = 0.5 * (imag_part - reflect(imag_part))
    return jnp.concatenate([real_part, imag_part], axis=-1)


def draw_state(key, part):
    return hermitian(jax.random.fold_in(key, 11))


def draw_accum(key, part):
    return hermitian(jax.random.fold_in(key, 23))


def levels(rng, extent, cuts, least, largest):
    def one(dim, shards_of):
        heights = jax.random.uniform(jax.random.fold_in(jax.random.fold_in(rng, 6), dim), (shards_of,), jnp.float32, least / len(cuts), largest / len(cuts))
        return jnp.repeat(jnp.exp(heights), extent[dim] // shards_of).reshape((-1,) + (1,) * (len(extent) - dim - 1))

    level = one(*cuts[0])
    for cut in cuts[1:]:
        level = level * one(*cut)
    return level


def noise(key, extent, width, bound, cuts=(), held_as=jnp.bfloat16):
    values = jax.random.normal(key, extent, jnp.float32) * width
    if len(cuts) > 0:
        values = levels(key, extent, cuts, -0.22, 0.18) * values
    return jnp.clip(values, min=-bound, max=bound).astype(held_as)


def setup_inputs(seed: int = 0) -> dict:
    seeds = jax.random.split(jax.random.key(seed), 4)
    state = draw_state(jax.random.fold_in(seeds[3], 71), 0)
    accum = draw_accum(jax.random.fold_in(seeds[3], 71), 0)
    base_flow = noise(seeds[2], (6, LEVELS, GRID, GRID), 1.0, 6.0, ((2, 16), (3, 32)), jnp.float32)
    return dict(state=state, accum=accum, base_flow=base_flow)


viscosity = 0.05
diffusivity = 0.05
vertical_mixing = 0.5
buoyancy_gain = 0.5
stratification = 0.5
memory_factor = -5.0 / 9.0
weight_factor = 15.0 / 16.0
time_step = 0.4


def wave_numbers(amount, offset, length):
    position = offset + jnp.arange(amount, dtype=jnp.int32)
    half_length = length // 2
    signed = jnp.where(position <= half_length, position, position - length)
    derivative = jnp.where(position == half_length, 0, signed)
    return (2.0 * math.pi / length) * derivative.astype(jnp.float32), signed


def times_i(real_part, imag_part, factor):
    return -factor * imag_part, factor * real_part


def vertical(quantity, level_axis):
    depth = quantity.shape[level_axis]
    lower = lax.slice_in_dim(quantity, 0, 1, axis=level_axis)
    upper = lax.slice_in_dim(quantity, depth - 1, depth, axis=level_axis)
    padded = jnp.concatenate([lower, quantity, upper], axis=level_axis)
    above = lax.slice_in_dim(padded, 2, depth + 2, axis=level_axis)
    below = lax.slice_in_dim(padded, 0, depth, axis=level_axis)
    return above + below - 2.0 * quantity


def tendency(vort, buoy, advect, across, kappa_x, square, level_axis):
    tend_vort_re = (-advect[0] + buoyancy_gain * (-kappa_x * buoy[1]) - viscosity * square * vort[0]
                    + vertical_mixing * vertical(vort[0], level_axis))
    tend_vort_im = (-advect[1] + buoyancy_gain * (kappa_x * buoy[0]) - viscosity * square * vort[1]
                    + vertical_mixing * vertical(vort[1], level_axis))
    tend_buoy_re = (-advect[2] - stratification * across[0] - diffusivity * square * buoy[0]
                    + vertical_mixing * vertical(buoy[0], level_axis))
    tend_buoy_im = (-advect[3] - stratification * across[1] - diffusivity * square * buoy[1]
                    + vertical_mixing * vertical(buoy[1], level_axis))
    return jnp.stack([jnp.concatenate([tend_vort_re, tend_vort_im], axis=-1),
                      jnp.concatenate([tend_buoy_re, tend_buoy_im], axis=-1)])


def physical(spectral_pair):
    joined = spectral_pair[0] + 1j * spectral_pair[1]
    return jnp.real(jnp.fft.ifft2(jnp.swapaxes(joined, -1, -2), norm="ortho"))


def spectrum(quantity):
    result = jnp.swapaxes(jnp.fft.fft2(quantity, norm="ortho"), -1, -2)
    return jnp.real(result), jnp.imag(result)


def reference(state, accum, base_flow):
    def one_member(member_pair):
        member, memory = member_pair
        kappa, signed = wave_numbers(GRID, 0, GRID)
        kappa_y = kappa[:, None]
        kappa_x = kappa[None, :]
        wave_square = signed[:, None] ** 2 + signed[None, :] ** 2
        factor = (2.0 * math.pi / GRID) ** 2
        square = factor * wave_square.astype(jnp.float32)
        inverse = jnp.where(wave_square > 0, 1.0 / (factor * jnp.maximum(wave_square, 1).astype(jnp.float32)), 0.0)
        vort = (member[0][..., :GRID], member[0][..., GRID:])
        buoy = (member[1][..., :GRID], member[1][..., GRID:])
        potential_re = -vort[0] * inverse
        potential_im = -vort[1] * inverse
        flow_x = times_i(potential_re, potential_im, -kappa_y)
        flow_y = times_i(potential_re, potential_im, kappa_x)
        vort_x = times_i(vort[0], vort[1], kappa_x)
        vort_y = times_i(vort[0], vort[1], kappa_y)
        buoy_x = times_i(buoy[0], buoy[1], kappa_x)
        buoy_y = times_i(buoy[0], buoy[1], kappa_y)
        flow_x_p = physical(flow_x)
        flow_y_p = physical(flow_y)
        vort_x_p = physical(vort_x)
        vort_y_p = physical(vort_y)
        buoy_x_p = physical(buoy_x)
        buoy_y_p = physical(buoy_y)
        advect_vort = (base_flow[0] * vort_x_p + base_flow[1] * vort_y_p
                       + flow_x_p * base_flow[2] + flow_y_p * base_flow[3])
        advect_buoy = (base_flow[0] * buoy_x_p + base_flow[1] * buoy_y_p
                       + flow_x_p * base_flow[4] + flow_y_p * base_flow[5])
        vort_hat = spectrum(advect_vort)
        buoy_hat = spectrum(advect_buoy)
        advect = (vort_hat[0], vort_hat[1], buoy_hat[0], buoy_hat[1])
        tend = tendency(vort, buoy, advect, flow_y, kappa_x, square, 0)
        memory_next = memory_factor * memory + tend
        return member + weight_factor * time_step * memory_next, memory_next

    members = (jnp.moveaxis(state, 1, 0), jnp.moveaxis(accum, 1, 0))
    state_next, accum_next = lax.map(one_member, members)
    return jnp.moveaxis(state_next, 0, 1), jnp.moveaxis(accum_next, 0, 1)
```

```python
import functools
import math

import jax
import jax.numpy as jnp
import numpy as np
from jax import lax
from jax.experimental import pallas as pl
from jax.experimental.pallas import tpu as pltpu
from jax.sharding import PartitionSpec as P

viscosity = 0.05
vertical_mixing = 0.5
buoyancy_gain = 0.5
stratification = 0.5
memory_factor = -5.0 / 9.0
weight_factor = 15.0 / 16.0
time_step = 0.4

GRID = 256
LEVELS = 4
ROWS = 16
PEN = 16
CHUNK = 64
MESH = pl.DeviceIdType.MESH
F32 = jnp.float32
BF16 = jnp.bfloat16


def halves(table):
    high = table.astype(np.float32).astype(jnp.bfloat16)
    low = (table - high.astype(np.float64)).astype(np.float32).astype(jnp.bfloat16)
    return np.stack([high, low])


def tables():
    position = np.arange(GRID)
    angle = 2.0 * np.pi / GRID * (position[:, None] * position[None, :] % GRID)
    cosine, sine = np.cos(angle) / 16.0, np.sin(angle) / 16.0
    x_inverse = np.stack([np.stack([cosine, sine], 1), np.stack([-sine, cosine], 1)])
    x_inverse = x_inverse.reshape(2, GRID, 2, GRID // CHUNK, CHUNK).transpose(0, 1, 3, 2, 4)
    x_inverse = x_inverse.reshape(2 * GRID, 2 * GRID)
    y_table = np.concatenate([cosine, sine])
    return halves(x_inverse), halves(y_table), halves(x_inverse.T.copy())


def split(value):
    high = value.astype(BF16)
    return high, (value - high.astype(F32)).astype(BF16)


def dot(a, b):
    return jnp.dot(a, b, preferred_element_type=F32)


def product(a, b):
    return dot(a[0], b[0]) + (dot(a[1], b[0]) + dot(a[0], b[1]))


def exact(a, b, dims):
    return lax.dot_general(
        a, b, (dims, ((), ())), precision=lax.Precision.HIGHEST, preferred_element_type=F32
    )


def wave_numbers(shape, dim, offset):
    position = lax.broadcasted_iota(jnp.int32, shape, dim) + offset
    signed = jnp.where(position <= GRID // 2, position, position - GRID)
    derivative = jnp.where(position == GRID // 2, 0, signed)
    return (2.0 * math.pi / GRID) * derivative.astype(F32), signed


def kernel(
    groups,
    state_hbm, accum_hbm, base_hbm, xt_hbm, yt_hbm, xf_hbm,
    state_next, accum_next,
    st, ac, bs, xt, yt, xf, xs, g, b0, b1, bb, ys, h, lin,
    load_sem, out_sem, fs, fr, rs, rr, as_, ar, cs, cr, hs, hr, own_sem,
):
    ens = lax.axis_index("ens")
    pen = lax.axis_index("pen")
    pair, core = ens // 2, ens % 2
    column, row = pen // 4, pen % 4
    other = ens + 1 - 2 * core
    rows_y = GRID // (2 * groups)

    barrier = pltpu.get_barrier_semaphore()
    for k in range(1, PEN):
        pl.semaphore_signal(barrier, inc=1, device_id=(ens, (pen + k) % PEN), device_id_type=MESH)
    for k in range(1, groups):
        pl.semaphore_signal(
            barrier, inc=1, device_id=((pair + k) % groups * 2 + core, pen), device_id_type=MESH
        )
    pl.semaphore_signal(barrier, inc=1, device_id=(other, pen), device_id_type=MESH)

    loads = [
        pltpu.make_async_copy(source, target, load_sem.at[i])
        for i, (source, target) in enumerate(
            [(base_hbm, bs), (state_hbm, st), (xt_hbm, xt), (accum_hbm, ac), (yt_hbm, yt), (xf_hbm, xf)]
        )
    ]
    for load in loads:
        load.start()

    loads[0].wait()
    unit = (
        lax.broadcasted_iota(jnp.int32, (rows_y, rows_y), 0)
        == lax.broadcasted_iota(jnp.int32, (rows_y, rows_y), 1)
    ).astype(F32)
    source_lane = lax.broadcasted_iota(jnp.int32, (96, 384), 0)
    place = (
        lax.broadcasted_iota(jnp.int32, (96, 384), 1)
        == source_lane // 16 * CHUNK + source_lane % 16 + row * 16
    ).astype(F32)
    for level in range(LEVELS):
        turned = exact(unit, bs[:, level].reshape(96, rows_y), ((1,), (1,)))
        b0[level] = exact(turned, place, ((1,), (0,)))

    kappa_y, signed_y = wave_numbers((ROWS, 1), 0, pen * ROWS)
    kappa_x, signed_x = wave_numbers((1, GRID), 1, 0)
    wave_square = signed_y * signed_y + signed_x * signed_x
    factor = (2.0 * math.pi / GRID) ** 2
    square = factor * wave_square.astype(F32)
    inverse = jnp.where(
        wave_square > 0, 1.0 / (factor * jnp.maximum(wave_square, 1).astype(F32)), 0.0
    )

    loads[1].wait()
    loads[2].wait()

    def transform_x(level):
        zr, zi = st[0, level, :, :GRID], st[0, level, :, GRID:]
        tr, ti = st[1, level, :, :GRID], st[1, level, :, GRID:]
        wzr, wzi = kappa_x * zr - kappa_y * zi, kappa_x * zi + kappa_y * zr
        wtr, wti = kappa_x * tr - kappa_y * ti, kappa_x * ti + kappa_y * tr
        packed = jnp.concatenate(
            [
                jnp.concatenate([wzr * inverse, wzi * inverse], axis=1),
                jnp.concatenate([-wzi, wzr], axis=1),
                jnp.concatenate([-wti, wtr], axis=1),
            ],
            axis=0,
        )
        mixed = product(split(packed), (xt[0], xt[1]))
        for c in range(4):
            xs[level, c] = mixed[:, 128 * c : 128 * (c + 1)].reshape(3, ROWS, 128)

    def forward(level, c):
        target = c * 4 + level
        return pltpu.make_async_remote_copy(
            src_ref=xs.at[level, c],
            dst_ref=g.at[pen],
            send_sem=fs.at[target],
            recv_sem=fr.at[pen],
            device_id=(ens, target),
            device_id_type=MESH,
        )

    def spread(k):
        target = column * 4 + (row + k) % 4
        return pltpu.make_async_remote_copy(
            src_ref=b0.at[(row + k) % 4],
            dst_ref=b1.at[row],
            send_sem=as_.at[(row + k) % 4],
            recv_sem=ar.at[row],
            device_id=(ens, target),
            device_id_type=MESH,
        )

    transform_x((row + 2) % 4)
    pl.semaphore_wait(barrier, PEN - 1 + groups - 1 + 1)
    for k in (2, 1, 3):
        spread(k).start()
    for step, k in enumerate((2, 1, 3, 0)):
        level = (row + k) % 4
        if step > 0:
            transform_x(level)
        for m in (2, 1, 3, 0):
            if k != 0 or m != 0:
                forward(level, (column + m) % 4).start()
    own = pltpu.make_async_copy(xs.at[row, column], g.at[pen], own_sem.at[0])
    own.start()

    def gather(k):
        target = (pair + k) % groups
        return pltpu.make_async_remote_copy(
            src_ref=bb.at[pair, core],
            dst_ref=bb.at[pair, core],
            send_sem=hs.at[target],
            recv_sem=hr.at[pair],
            device_id=(target * 2 + core, pen),
            device_id_type=MESH,
        )

    def gathered(k):
        source = (pair + k) % groups
        return pltpu.make_async_remote_copy(
            src_ref=bb.at[source, core],
            dst_ref=bb.at[source, core],
            send_sem=hs.at[source],
            recv_sem=hr.at[source],
            device_id=(source * 2 + core, pen),
            device_id_type=MESH,
        )

    def spread_from(k):
        source = (row + k) % 4
        return pltpu.make_async_remote_copy(
            src_ref=b0.at[source],
            dst_ref=b1.at[source],
            send_sem=as_.at[source],
            recv_sem=ar.at[source],
            device_id=(ens, column * 4 + source),
            device_id_type=MESH,
        )

    b1[row] = b0[row]
    for k in range(1, 4):
        spread_from(k).wait_recv()
    bb[pair, core] = (b1[0] + b1[1]) + (b1[2] + b1[3])
    for k in range(1, groups):
        gather(k).start()

    loads[3].wait()
    for level in range(LEVELS):
        up, down = min(level + 1, LEVELS - 1), max(level - 1, 0)
        zr, zi = st[0, level, :, :GRID], st[0, level, :, GRID:]
        tr, ti = st[1, level, :, :GRID], st[1, level, :, GRID:]
        across = stratification * kappa_x * inverse
        linear = (
            jnp.concatenate([-buoyancy_gain * kappa_x * ti, buoyancy_gain * kappa_x * tr], axis=1),
            jnp.concatenate([-across * zi, across * zr], axis=1),
        )
        damping = viscosity * jnp.concatenate([square, square], axis=1)
        for field in range(2):
            value = st[field, level]
            mixing = st[field, up] + st[field, down] - 2.0 * value
            lin[field, level] = (
                memory_factor * ac[field, level]
                + linear[field]
                - damping * value
                + vertical_mixing * mixing
            )

    for k in range(1, groups):
        gathered(k).wait_recv()
    swap = pltpu.make_async_remote_copy(
        src_ref=bb.at[:, core],
        dst_ref=bb.at[:, core],
        send_sem=cs.at[0],
        recv_sem=cr.at[0],
        device_id=(other, pen),
        device_id_type=MESH,
    )
    swap.start()

    loads[4].wait()
    own.wait()

    def forward_from(k):
        source = (pen + k) % PEN
        return pltpu.make_async_remote_copy(
            src_ref=xs.at[source % 4, source // 4],
            dst_ref=g.at[source],
            send_sem=fs.at[source],
            recv_sem=fr.at[source],
            device_id=(ens, source),
            device_id_type=MESH,
        )

    for k in range(1, PEN):
        forward_from(k).wait_recv()

    table = (yt[0], yt[1])
    spectral = jnp.concatenate([g[:, f].reshape(GRID, 128) for f in range(3)], axis=1)
    turned = product(table, split(spectral))
    lane = lax.broadcasted_iota(jnp.int32, (1, 128), 1)
    first = lane < CHUNK
    sign = jnp.where(first, -1.0, 1.0)

    def swap_halves(value):
        return pltpu.roll(value, CHUNK, 1)

    physical = []
    for f in range(3):
        even = turned[:GRID, 128 * f : 128 * (f + 1)]
        odd = turned[GRID:, 128 * f : 128 * (f + 1)]
        physical.append(even + sign * swap_halves(odd))

    pltpu.make_async_remote_copy(
        src_ref=bb.at[:, 1 - core],
        dst_ref=bb.at[:, 1 - core],
        send_sem=cs.at[0],
        recv_sem=cr.at[0],
        device_id=(other, pen),
        device_id_type=MESH,
    ).wait_recv()
    base = bb[...].reshape(GRID, 384)
    flow, vort_slope, buoy_slope = base[:, :128], base[:, 128:256], base[:, 256:]
    advect_vort = flow * physical[1] + vort_slope * physical[0]
    advect_buoy = flow * physical[2] + buoy_slope * physical[0]
    advect = jnp.where(
        first, advect_vort + swap_halves(advect_vort), advect_buoy + swap_halves(advect_buoy)
    )
    spread_y = product(table, split(advect))
    real, imag = spread_y[:GRID], -spread_y[GRID:]
    ys[:, 0] = jnp.where(first, real, swap_halves(imag)).reshape(PEN, ROWS, 128)
    ys[:, 1] = jnp.where(first, swap_halves(real), imag).reshape(PEN, ROWS, 128)

    def backward(target):
        return pltpu.make_async_remote_copy(
            src_ref=ys.at[target],
            dst_ref=h.at[pen],
            send_sem=rs.at[target],
            recv_sem=rr.at[pen],
            device_id=(ens, target),
            device_id_type=MESH,
        )

    def backward_from(source):
        return pltpu.make_async_remote_copy(
            src_ref=ys.at[source],
            dst_ref=h.at[source],
            send_sem=rs.at[source],
            recv_sem=rr.at[source],
            device_id=(ens, source),
            device_id_type=MESH,
        )

    for k in (2, 1, 3, 0):
        for m in (2, 1, 3, 0):
            if k != 0 or m != 0:
                backward((column + m) % 4 * 4 + (row + k) % 4).start()
    h[pen] = ys[pen]
    loads[5].wait()
    for k in range(1, PEN):
        backward_from((pen + k) % PEN).wait_recv()

    gathered_x = jnp.concatenate([h[4 * c : 4 * c + 4].reshape(128, 128) for c in range(4)], axis=1)
    spectra = product(split(gathered_x), (xf[0], xf[1]))
    step = weight_factor * time_step
    for level in range(LEVELS):
        for field in range(2):
            start = (level * 2 + field) * ROWS
            value = lin[field, level] - spectra[start : start + ROWS]
            lin[field, level] = value
            st[field, level] = st[field, level] + step * value
    outs = [
        pltpu.make_async_copy(lin, accum_next, out_sem.at[0]),
        pltpu.make_async_copy(st, state_next, out_sem.at[1]),
    ]
    for out in outs:
        out.start()

    for k in (1, 2, 3):
        spread_from(k).wait_send()
    for k in range(1, groups):
        gathered(k).wait_send()
    swap.wait_send()
    for k in range(1, PEN):
        forward_from(k).wait_send()
        backward_from((pen + k) % PEN).wait_send()
    for out in outs:
        out.wait()


def on_device(groups, state, accum, base_flow):
    rows_y = GRID // (2 * groups)
    x_inverse, y_table, x_forward = tables()
    fields = (2, LEVELS, ROWS, 2 * GRID)
    result = jax.ShapeDtypeStruct(fields, F32)
    dma = pltpu.SemaphoreType.DMA
    outputs = pl.pallas_call(
        functools.partial(kernel, groups),
        out_shape=(result, result),
        in_specs=[pl.BlockSpec(memory_space=pl.ANY)] * 6,
        out_specs=(pl.BlockSpec(memory_space=pl.ANY),) * 2,
        scratch_shapes=[
            pltpu.VMEM(fields, F32),
            pltpu.VMEM(fields, F32),
            pltpu.VMEM((6, LEVELS, 16, rows_y), F32),
            pltpu.VMEM((2, 2 * GRID, 2 * GRID), BF16),
            pltpu.VMEM((2, 2 * GRID, GRID), BF16),
            pltpu.VMEM((2, 2 * GRID, 2 * GRID), BF16),
            pltpu.VMEM((LEVELS, 4, 3, ROWS, 128), F32),
            pltpu.VMEM((PEN, 3, ROWS, 128), F32),
            pltpu.VMEM((LEVELS, rows_y, 384), F32),
            pltpu.VMEM((4, rows_y, 384), F32),
            pltpu.VMEM((groups, 2, rows_y, 384), F32),
            pltpu.VMEM((PEN, 2, ROWS, 128), F32),
            pltpu.VMEM((PEN, 2, ROWS, 128), F32),
            pltpu.VMEM(fields, F32),
            dma((6,)),
            dma((2,)),
            dma((PEN,)),
            dma((PEN,)),
            dma((PEN,)),
            dma((PEN,)),
            dma((4,)),
            dma((4,)),
            dma((1,)),
            dma((1,)),
            dma((groups,)),
            dma((groups,)),
            dma((1,)),
        ],
        compiler_params=pltpu.CompilerParams(
            collective_id=0, has_side_effects=True, vmem_limit_bytes=40 * 1024 * 1024
        ),
        name="step",
    )(
        state.reshape(fields), accum.reshape(fields), base_flow,
        jnp.asarray(x_inverse), jnp.asarray(y_table), jnp.asarray(x_forward),
    )
    return tuple(out.reshape(state.shape) for out in outputs)


def solution(mesh):
    spectral = P(None, "ens", None, "pen", None)
    return jax.shard_map(
        functools.partial(on_device, mesh.shape["ens"] // 2),
        mesh=mesh,
        in_specs=(spectral, spectral, P(None, None, "pen", "ens")),
        out_specs=(spectral, spectral),
        check_vma=False,
    )
```

```python
import functools
import math

import jax
import jax.numpy as jnp
import numpy as np
from jax import lax
from jax.experimental import pallas as pl
from jax.experimental.pallas import tpu as pltpu
from jax.sharding import PartitionSpec as P

viscosity = 0.05
vertical_mixing = 0.5
buoyancy_gain = 0.5
stratification = 0.5
memory_factor = -5.0 / 9.0
weight_factor = 15.0 / 16.0
time_step = 0.4

GRID = 256
LEVELS = 4
ROWS = 16
PEN = 16
CHUNK = 64
MESH = pl.DeviceIdType.MESH
F32 = jnp.float32
BF16 = jnp.bfloat16


def halves(table):
    high = table.astype(np.float32).astype(jnp.bfloat16)
    low = (table - high.astype(np.float64)).astype(np.float32).astype(jnp.bfloat16)
    return np.stack([high, low])


def tables():
    position = np.arange(GRID)
    angle = 2.0 * np.pi / GRID * (position[:, None] * position[None, :] % GRID)
    table = np.stack([np.cos(angle), np.sin(angle)], 1).reshape(GRID, 2, GRID // CHUNK, CHUNK)
    table = table.transpose(0, 2, 1, 3).reshape(GRID, 2 * GRID) / 16.0
    return halves(table), halves(table.T.copy())


def split(value):
    high = value.astype(BF16)
    return high, (value - high.astype(F32)).astype(BF16)


def dot(a, b):
    return jnp.dot(a, b, preferred_element_type=F32)


def product(a, b):
    return dot(a[0], b[0]) + (dot(a[1], b[0]) + dot(a[0], b[1]))


def wave_numbers(shape, dim, offset):
    position = lax.broadcasted_iota(jnp.int32, shape, dim) + offset
    signed = jnp.where(position <= GRID // 2, position, position - GRID)
    derivative = jnp.where(position == GRID // 2, 0, signed)
    return (2.0 * math.pi / GRID) * derivative.astype(F32), signed


def kernel(
    groups,
    state_hbm, accum_hbm, base_hbm, wide_hbm, tall_hbm,
    state_next, accum_next,
    st, ac, bs, wide, tall, xs, g, b0, b1, bb, ys, h, lin,
    load_sem, fs, fr, rs, rr, as_, ar, cs, cr, hs, hr, own_sem,
):
    ens = lax.axis_index("ens")
    pen = lax.axis_index("pen")
    pair, core = ens // 2, ens % 2
    column, row = pen // 4, pen % 4
    other = ens + 1 - 2 * core
    rows_y = GRID // (2 * groups)

    barrier = pltpu.get_barrier_semaphore()
    for k in range(1, PEN):
        pl.semaphore_signal(barrier, inc=1, device_id=(ens, (pen + k) % PEN), device_id_type=MESH)
    for k in range(1, groups):
        pl.semaphore_signal(
            barrier, inc=1, device_id=((pair + k) % groups * 2 + core, pen), device_id_type=MESH
        )
    pl.semaphore_signal(barrier, inc=1, device_id=(other, pen), device_id_type=MESH)

    loads = [
        pltpu.make_async_copy(source, target, load_sem.at[i])
        for i, (source, target) in enumerate(
            [(base_hbm, bs), (state_hbm, st), (wide_hbm, wide), (tall_hbm, tall), (accum_hbm, ac)]
        )
    ]
    for load in loads:
        load.start()

    lane = lax.broadcasted_iota(jnp.int32, (1, 128), 1)
    first = lane < CHUNK
    sign = jnp.where(first, -1.0, 1.0)

    def swap_halves(value):
        return pltpu.roll(value, CHUNK, 1)

    loads[0].wait()
    place = (
        lax.broadcasted_iota(jnp.int32, (16, 128), 1) % CHUNK
        == lax.broadcasted_iota(jnp.int32, (16, 128), 0) + row * 16
    ).astype(F32)
    placed = lax.dot_general(
        bs[...].reshape(6 * LEVELS * rows_y, 16), place, (((1,), (0,)), ((), ())),
        precision=lax.Precision.HIGHEST, preferred_element_type=F32,
    ).reshape(6, LEVELS, rows_y, 128)
    for q in range(3):
        for level in range(LEVELS):
            b0[level, :, 128 * q : 128 * (q + 1)] = jnp.where(
                first, placed[2 * q, level], placed[2 * q + 1, level]
            )

    kappa_y, signed_y = wave_numbers((ROWS, 1), 0, pen * ROWS)
    kappa_x, signed_x = wave_numbers((1, GRID), 1, 0)
    wave_square = signed_y * signed_y + signed_x * signed_x
    factor = (2.0 * math.pi / GRID) ** 2
    square = factor * wave_square.astype(F32)
    inverse = jnp.where(
        wave_square > 0, 1.0 / (factor * jnp.maximum(wave_square, 1).astype(F32)), 0.0
    )

    loads[1].wait()
    loads[2].wait()

    def transform_x(level):
        zr, zi = st[0, level, :, :GRID], st[0, level, :, GRID:]
        tr, ti = st[1, level, :, :GRID], st[1, level, :, GRID:]
        wzr, wzi = kappa_x * zr - kappa_y * zi, kappa_x * zi + kappa_y * zr
        wtr, wti = kappa_x * tr - kappa_y * ti, kappa_x * ti + kappa_y * tr
        packed = jnp.concatenate(
            [wzr * inverse, -wzi, -wti, wzi * inverse, wzr, wtr], axis=0
        )
        mixed = product(split(packed), (wide[0], wide[1]))
        for c in range(4):
            even = mixed[: 3 * ROWS, 128 * c : 128 * (c + 1)]
            odd = mixed[3 * ROWS :, 128 * c : 128 * (c + 1)]
            xs[level, c] = (even + sign * swap_halves(odd)).reshape(3, ROWS, 128)

    def forward(level, c):
        target = c * 4 + level
        return pltpu.make_async_remote_copy(
            src_ref=xs.at[level, c],
            dst_ref=g.at[pen],
            send_sem=fs.at[target],
            recv_sem=fr.at[pen],
            device_id=(ens, target),
            device_id_type=MESH,
        )

    def spread(k):
        target = column * 4 + (row + k) % 4
        return pltpu.make_async_remote_copy(
            src_ref=b0.at[(row + k) % 4],
            dst_ref=b1.at[row],
            send_sem=as_.at[(row + k) % 4],
            recv_sem=ar.at[row],
            device_id=(ens, target),
            device_id_type=MESH,
        )

    transform_x((row + 2) % 4)
    pl.semaphore_wait(barrier, PEN - 1 + groups - 1 + 1)
    for k in (2, 1, 3):
        spread(k).start()
    for step, k in enumerate((2, 1, 3, 0)):
        level = (row + k) % 4
        if step > 0:
            transform_x(level)
        for m in (2, 1, 3, 0):
            if k != 0 or m != 0:
                forward(level, (column + m) % 4).start()
    own = pltpu.make_async_copy(xs.at[row, column], g.at[pen], own_sem.at[0])
    own.start()

    def gather(k):
        target = (pair + k) % groups
        return pltpu.make_async_remote_copy(
            src_ref=bb.at[pair, core],
            dst_ref=bb.at[pair, core],
            send_sem=hs.at[target],
            recv_sem=hr.at[pair],
            device_id=(target * 2 + core, pen),
            device_id_type=MESH,
        )

    def gathered(k):
        source = (pair + k) % groups
        return pltpu.make_async_remote_copy(
            src_ref=bb.at[source, core],
            dst_ref=bb.at[source, core],
            send_sem=hs.at[source],
            recv_sem=hr.at[source],
            device_id=(source * 2 + core, pen),
            device_id_type=MESH,
        )

    def spread_from(k):
        source = (row + k) % 4
        return pltpu.make_async_remote_copy(
            src_ref=b0.at[source],
            dst_ref=b1.at[source],
            send_sem=as_.at[source],
            recv_sem=ar.at[source],
            device_id=(ens, column * 4 + source),
            device_id_type=MESH,
        )

    b1[row] = b0[row]
    for k in range(1, 4):
        spread_from(k).wait_recv()
    bb[pair, core] = (b1[0] + b1[1]) + (b1[2] + b1[3])
    for k in range(1, groups):
        gather(k).start()

    loads[4].wait()
    for level in range(LEVELS):
        up, down = min(level + 1, LEVELS - 1), max(level - 1, 0)
        zr, zi = st[0, level, :, :GRID], st[0, level, :, GRID:]
        tr, ti = st[1, level, :, :GRID], st[1, level, :, GRID:]
        across = stratification * kappa_x * inverse
        linear = (
            jnp.concatenate([-buoyancy_gain * kappa_x * ti, buoyancy_gain * kappa_x * tr], axis=1),
            jnp.concatenate([-across * zi, across * zr], axis=1),
        )
        damping = viscosity * jnp.concatenate([square, square], axis=1)
        for field in range(2):
            value = st[field, level]
            mixing = st[field, up] + st[field, down] - 2.0 * value
            lin[field, level] = (
                memory_factor * ac[field, level]
                + linear[field]
                - damping * value
                + vertical_mixing * mixing
            )

    for k in range(1, groups):
        gathered(k).wait_recv()
    swap = pltpu.make_async_remote_copy(
        src_ref=bb.at[:, core],
        dst_ref=bb.at[:, core],
        send_sem=cs.at[0],
        recv_sem=cr.at[0],
        device_id=(other, pen),
        device_id_type=MESH,
    )
    swap.start()

    own.wait()

    def forward_from(k):
        source = (pen + k) % PEN
        return pltpu.make_async_remote_copy(
            src_ref=xs.at[source % 4, source // 4],
            dst_ref=g.at[source],
            send_sem=fs.at[source],
            recv_sem=fr.at[source],
            device_id=(ens, source),
            device_id_type=MESH,
        )

    for k in range(1, PEN):
        forward_from(k).wait_recv()

    loads[3].wait()
    table = (tall[0], tall[1])
    spectral = jnp.concatenate([g[:, f].reshape(GRID, 128) for f in range(3)], axis=1)
    turned = product(table, split(spectral))
    def blocks(value, part):
        return jnp.concatenate(
            [value[128 * c + CHUNK * part : 128 * c + CHUNK * (part + 1)] for c in range(4)], axis=0
        )

    physical = []
    for f in range(3):
        one = turned[:, 128 * f : 128 * (f + 1)]
        physical.append(blocks(one, 0) + sign * swap_halves(blocks(one, 1)))

    pltpu.make_async_remote_copy(
        src_ref=bb.at[:, 1 - core],
        dst_ref=bb.at[:, 1 - core],
        send_sem=cs.at[0],
        recv_sem=cr.at[0],
        device_id=(other, pen),
        device_id_type=MESH,
    ).wait_recv()
    base = bb[...].reshape(GRID, 384)
    flow, vort_slope, buoy_slope = base[:, :128], base[:, 128:256], base[:, 256:]
    advect_vort = flow * physical[1] + vort_slope * physical[0]
    advect_buoy = flow * physical[2] + buoy_slope * physical[0]
    advect = jnp.where(
        first, advect_vort + swap_halves(advect_vort), advect_buoy + swap_halves(advect_buoy)
    )
    spread_y = product(table, split(advect))
    real, imag = blocks(spread_y, 0), -blocks(spread_y, 1)
    ys[:, 0] = jnp.where(first, real, swap_halves(imag)).reshape(PEN, ROWS, 128)
    ys[:, 1] = jnp.where(first, swap_halves(real), imag).reshape(PEN, ROWS, 128)

    def backward(target):
        return pltpu.make_async_remote_copy(
            src_ref=ys.at[target],
            dst_ref=h.at[pen],
            send_sem=rs.at[target],
            recv_sem=rr.at[pen],
            device_id=(ens, target),
            device_id_type=MESH,
        )

    def backward_from(source):
        return pltpu.make_async_remote_copy(
            src_ref=ys.at[source],
            dst_ref=h.at[source],
            send_sem=rs.at[source],
            recv_sem=rr.at[source],
            device_id=(ens, source),
            device_id_type=MESH,
        )

    for k in (2, 1, 3, 0):
        for m in (2, 1, 3, 0):
            if k != 0 or m != 0:
                backward((column + m) % 4 * 4 + (row + k) % 4).start()
    h[pen] = ys[pen]
    for k in range(1, PEN):
        backward_from((pen + k) % PEN).wait_recv()

    chunks = [h[4 * c : 4 * c + 4].reshape(128, 128) for c in range(4)]
    gathered_x = jnp.concatenate(
        [jnp.concatenate(chunks, axis=1),
         jnp.concatenate([-sign * swap_halves(chunk) for chunk in chunks], axis=1)], axis=0
    )
    spectra = product(split(gathered_x), table)
    step = weight_factor * time_step
    for level in range(LEVELS):
        for field in range(2):
            start = (level * 2 + field) * ROWS
            for part in range(2):
                at = slice(GRID * part, GRID * (part + 1))
                value = lin[field, level, :, at] - spectra[128 * part + start : 128 * part + start + ROWS]
                accum_next[field, level, :, at] = value
                state_next[field, level, :, at] = st[field, level, :, at] + step * value

    for k in (1, 2, 3):
        spread_from(k).wait_send()
    for k in range(1, groups):
        gathered(k).wait_send()
    swap.wait_send()
    for k in range(1, PEN):
        forward_from(k).wait_send()
        backward_from((pen + k) % PEN).wait_send()


def on_device(groups, state, accum, base_flow):
    rows_y = GRID // (2 * groups)
    wide, tall = tables()
    fields = (2, LEVELS, ROWS, 2 * GRID)
    result = jax.ShapeDtypeStruct(fields, F32)
    dma = pltpu.SemaphoreType.DMA
    outputs = pl.pallas_call(
        functools.partial(kernel, groups),
        out_shape=(result, result),
        in_specs=[pl.BlockSpec(memory_space=pltpu.HBM)] * 5,
        out_specs=(pl.BlockSpec(memory_space=pltpu.VMEM),) * 2,
        scratch_shapes=[
            pltpu.VMEM(fields, F32),
            pltpu.VMEM(fields, F32),
            pltpu.VMEM((6, LEVELS, rows_y, 16), F32),
            pltpu.VMEM((2, GRID, 2 * GRID), BF16),
            pltpu.VMEM((2, 2 * GRID, GRID), BF16),
            pltpu.VMEM((LEVELS, 4, 3, ROWS, 128), F32),
            pltpu.VMEM((PEN, 3, ROWS, 128), F32),
            pltpu.VMEM((LEVELS, rows_y, 384), F32),
            pltpu.VMEM((4, rows_y, 384), F32),
            pltpu.VMEM((groups, 2, rows_y, 384), F32),
            pltpu.VMEM((PEN, 2, ROWS, 128), F32),
            pltpu.VMEM((PEN, 2, ROWS, 128), F32),
            pltpu.VMEM(fields, F32),
            dma((5,)),
            dma((PEN,)),
            dma((PEN,)),
            dma((PEN,)),
            dma((PEN,)),
            dma((4,)),
            dma((4,)),
            dma((1,)),
            dma((1,)),
            dma((groups,)),
            dma((groups,)),
            dma((1,)),
        ],
        compiler_params=pltpu.CompilerParams(
            collective_id=0, has_side_effects=True, vmem_limit_bytes=40 * 1024 * 1024
        ),
        name="step",
    )(*[pltpu.with_memory_space_constraint(x, pltpu.HBM) for x in (
        state.reshape(fields), accum.reshape(fields), base_flow.transpose(0, 1, 3, 2),
        jnp.asarray(wide), jnp.asarray(tall))]
    )
    return tuple(out.reshape(state.shape) for out in outputs)


def solution(mesh):
    spectral = P(None, "ens", None, "pen", None)
    return jax.shard_map(
        functools.partial(on_device, mesh.shape["ens"] // 2),
        mesh=mesh,
        in_specs=(spectral, spectral, P(None, None, "pen", "ens")),
        out_specs=(spectral, spectral),
        check_vma=False,
    )
```

```python
import functools
import math

import jax
import jax.numpy as jnp
import numpy as np
from jax import lax
from jax.experimental import pallas as pl
from jax.experimental.pallas import tpu as pltpu
from jax.sharding import PartitionSpec as P

viscosity = 0.05
vertical_mixing = 0.5
buoyancy_gain = 0.5
stratification = 0.5
memory_factor = -5.0 / 9.0
weight_factor = 15.0 / 16.0
time_step = 0.4

GRID = 256
LEVELS = 4
ROWS = 16
PEN = 16
CHUNK = 16
MESH = pl.DeviceIdType.MESH
F32 = jnp.float32
BF16 = jnp.bfloat16


def halves(table):
    high = table.astype(np.float32).astype(jnp.bfloat16)
    low = (table - high.astype(np.float64)).astype(np.float32).astype(jnp.bfloat16)
    return np.stack([high, low])


def tables():
    position = np.arange(GRID)
    angle = 2.0 * np.pi / GRID * (position[:, None] * position[None, :] % GRID)
    table = np.stack([np.cos(angle), np.sin(angle)], 1).reshape(GRID, 2, GRID // CHUNK, CHUNK)
    table = table.transpose(0, 2, 1, 3).reshape(GRID, 2 * GRID) / 16.0
    return halves(table), halves(table.T.copy())


def split(value):
    high = value.astype(BF16)
    return high, (value - high.astype(F32)).astype(BF16)


def dot(a, b):
    return jnp.dot(a, b, preferred_element_type=F32)


def product(a, b):
    return dot(a[0], b[0]) + (dot(a[1], b[0]) + dot(a[0], b[1]))


def wave_numbers(shape, dim, offset):
    position = lax.broadcasted_iota(jnp.int32, shape, dim) + offset
    signed = jnp.where(position <= GRID // 2, position, position - GRID)
    derivative = jnp.where(position == GRID // 2, 0, signed)
    return (2.0 * math.pi / GRID) * derivative.astype(F32), signed


def kernel(
    groups,
    state_hbm, accum_hbm, base_hbm, wide_hbm, tall_hbm,
    state_next, accum_next,
    st, ac, bs, wide, tall, pk_high, pk_low, xs, g, bb, ys, h, lin,
    load_sem, fs, fr, rs, rr, cs, cr, hs, hr, own_sem, here,
):
    ens = lax.axis_index("ens")
    pen = lax.axis_index("pen")
    pair, core = ens // 2, ens % 2
    column, row = pen // 4, pen % 4
    other = ens + 1 - 2 * core
    rows_y = GRID // (2 * groups)

    barrier = pltpu.get_barrier_semaphore()
    for k in range(1, PEN):
        pl.semaphore_signal(barrier, inc=1, device_id=(ens, (pen + k) % PEN), device_id_type=MESH)
    pl.semaphore_signal(barrier, inc=1, device_id=(other, pen), device_id_type=MESH)
    for k in range(1, groups):

        @pl.when(pair + k < groups)
        def _():
            pl.semaphore_signal(
                barrier, inc=1, device_id=((pair + k) * 2 + core, pen), device_id_type=MESH
            )

    loads = [
        pltpu.make_async_copy(source, target, load_sem.at[i])
        for i, (source, target) in enumerate(
            [(base_hbm, bs), (state_hbm, st), (wide_hbm, wide), (tall_hbm, tall), (accum_hbm, ac)]
        )
    ]
    for load in loads:
        load.start()

    lane = lax.broadcasted_iota(jnp.int32, (1, 128), 1)
    first = lane // CHUNK % 2 == 0
    sign = jnp.where(first, -1.0, 1.0)

    def swap_parts(value):
        return jnp.where(
            first, pltpu.roll(value, 128 - CHUNK, 1), pltpu.roll(value, CHUNK, 1)
        )

    def turn(values):
        results = []
        for j in range(4):
            result = None
            for l in range(4):
                moved = values[l] if l == j else pltpu.roll(values[l], 32 * (l - j) % 128, 1)
                result = moved if result is None else jnp.where(lane // 32 == l, moved, result)
            results.append(result)
        return results

    loads[0].wait()
    place = (
        lax.broadcasted_iota(jnp.int32, (CHUNK, 128), 1) % CHUNK
        == lax.broadcasted_iota(jnp.int32, (CHUNK, 128), 0)
    ).astype(F32)
    placed = lax.dot_general(
        bs[...].reshape(6 * LEVELS * rows_y, CHUNK), place, (((1,), (0,)), ((), ())),
        precision=lax.Precision.HIGHEST, preferred_element_type=F32,
    ).reshape(6, LEVELS, rows_y, 128)
    for q in range(3):
        result = placed[2 * q, 0]
        for group in range(1, 8):
            result = jnp.where(
                lane // CHUNK == group, placed[2 * q + group % 2, group // 2], result
            )
        bb[pair, core, :, 128 * q : 128 * (q + 1)] = result

    def gather(target):
        return pltpu.make_async_remote_copy(
            src_ref=bb.at[pair, core],
            dst_ref=bb.at[pair, core],
            send_sem=hs.at[target],
            recv_sem=hr.at[pair],
            device_id=(target * 2 + core, pen),
            device_id_type=MESH,
        )

    def gathered(source):
        return pltpu.make_async_remote_copy(
            src_ref=bb.at[source, core],
            dst_ref=bb.at[source, core],
            send_sem=hs.at[source],
            recv_sem=hr.at[source],
            device_id=(source * 2 + core, pen),
            device_id_type=MESH,
        )

    pl.semaphore_wait(barrier, PEN + pair)
    for k in range(1, groups):

        @pl.when(pair - k >= 0)
        def _():
            pl.semaphore_signal(
                here.at[pair], inc=1, device_id=((pair - k) * 2 + core, pen), device_id_type=MESH
            )
            gather(pair - k).start()

    kappa_y, signed_y = wave_numbers((ROWS, 1), 0, pen * ROWS)
    kappa_x, signed_x = wave_numbers((1, GRID), 1, 0)
    wave_square = signed_y * signed_y + signed_x * signed_x
    factor = (2.0 * math.pi / GRID) ** 2
    square = factor * wave_square.astype(F32)
    inverse = jnp.where(
        wave_square > 0, 1.0 / (factor * jnp.maximum(wave_square, 1).astype(F32)), 0.0
    )

    loads[1].wait()
    loads[2].wait()

    packed = []
    for level in range(LEVELS):
        zr, zi = st[0, level, :, :GRID], st[0, level, :, GRID:]
        tr, ti = st[1, level, :, :GRID], st[1, level, :, GRID:]
        wzr, wzi = kappa_x * zr - kappa_y * zi, kappa_x * zi + kappa_y * zr
        wtr, wti = kappa_x * tr - kappa_y * ti, kappa_x * ti + kappa_y * tr
        packed += [wzr * inverse, -wzi, -wti, wzi * inverse, wzr, wtr]
    pk_high[...], pk_low[...] = split(jnp.concatenate(packed, axis=0))

    def forward(target):
        return pltpu.make_async_remote_copy(
            src_ref=xs.at[target],
            dst_ref=g.at[pen],
            send_sem=fs.at[target],
            recv_sem=fr.at[pen],
            device_id=(ens, target),
            device_id_type=MESH,
        )

    for m in (2, 1, 3, 0):
        to = (column + m) % 4
        at = pl.ds(pl.multiple_of(to * 128, 128), 128)
        mixed = product((pk_high[...], pk_low[...]), (wide[0, :, at], wide[1, :, at]))
        mixed = mixed.reshape(LEVELS, 2, 3 * ROWS, 128)
        parts = turn([mixed[l, 0] + sign * swap_parts(mixed[l, 1]) for l in range(LEVELS)])
        for j in range(4):
            xs[to * 4 + j] = parts[j].reshape(3, ROWS, 128)
        for k in (2, 1, 3, 0):
            if k != 0 or m != 0:
                forward(to * 4 + (row + k) % 4).start()
    own = pltpu.make_async_copy(xs.at[pen], g.at[pen], own_sem.at[0])
    own.start()
    for k in range(1, groups):

        @pl.when(pair + k < groups)
        def _():
            pl.semaphore_wait(here.at[pair + k], 1)
            gather(pair + k).start()

    loads[4].wait()
    for level in range(LEVELS):
        up, down = min(level + 1, LEVELS - 1), max(level - 1, 0)
        zr, zi = st[0, level, :, :GRID], st[0, level, :, GRID:]
        tr, ti = st[1, level, :, :GRID], st[1, level, :, GRID:]
        across = stratification * kappa_x * inverse
        linear = (
            jnp.concatenate([-buoyancy_gain * kappa_x * ti, buoyancy_gain * kappa_x * tr], axis=1),
            jnp.concatenate([-across * zi, across * zr], axis=1),
        )
        damping = viscosity * jnp.concatenate([square, square], axis=1)
        for field in range(2):
            value = st[field, level]
            mixing = st[field, up] + st[field, down] - 2.0 * value
            lin[field, level] = (
                memory_factor * ac[field, level]
                + linear[field]
                - damping * value
                + vertical_mixing * mixing
            )

    half = groups // 2

    def swap(part, side):
        return pltpu.make_async_remote_copy(
            src_ref=bb.at[half * part : half * (part + 1), side],
            dst_ref=bb.at[half * part : half * (part + 1), side],
            send_sem=cs.at[part],
            recv_sem=cr.at[part],
            device_id=(other, pen),
            device_id_type=MESH,
        )

    for part in range(2):
        for source in range(half * part, half * (part + 1)):

            @pl.when(pair != source)
            def _():
                gathered(source).wait_recv()

        swap(part, core).start()

    own.wait()

    def forward_from(k):
        source = (pen + k) % PEN
        return pltpu.make_async_remote_copy(
            src_ref=xs.at[source],
            dst_ref=g.at[source],
            send_sem=fs.at[source],
            recv_sem=fr.at[source],
            device_id=(ens, source),
            device_id_type=MESH,
        )

    for k in range(1, PEN):
        forward_from(k).wait_recv()

    loads[3].wait()
    table = (tall[0], tall[1])
    spectral = jnp.concatenate([g[:, f].reshape(GRID, 128) for f in range(3)], axis=1)
    turned = product(table, split(spectral))
    def blocks(value, part):
        rows = value.reshape(value.shape[0] // 32, 2, CHUNK, 128)[:, part]
        return rows.reshape(value.shape[0] // 2, 128)

    physical = []
    for f in range(3):
        one = turned[:, 128 * f : 128 * (f + 1)]
        physical.append(blocks(one, 0) + sign * swap_parts(blocks(one, 1)))

    for part in range(2):
        swap(part, 1 - core).wait_recv()
    base = bb[...].reshape(GRID, 384)
    flow, vort_slope, buoy_slope = base[:, :128], base[:, 128:256], base[:, 256:]
    advect_vort = flow * physical[1] + vort_slope * physical[0]
    advect_buoy = flow * physical[2] + buoy_slope * physical[0]
    advect = jnp.where(
        first, advect_vort + swap_parts(advect_vort), advect_buoy + swap_parts(advect_buoy)
    )
    adverse = split(advect)

    def backward(target):
        return pltpu.make_async_remote_copy(
            src_ref=ys.at[target],
            dst_ref=h.at[pen],
            send_sem=rs.at[target],
            recv_sem=rr.at[pen],
            device_id=(ens, target),
            device_id_type=MESH,
        )

    def backward_from(source):
        return pltpu.make_async_remote_copy(
            src_ref=ys.at[source],
            dst_ref=h.at[source],
            send_sem=rs.at[source],
            recv_sem=rr.at[source],
            device_id=(ens, source),
            device_id_type=MESH,
        )

    for m in (2, 1, 3, 0):
        to = (column + m) % 4
        rows = pl.ds(pl.multiple_of(to * 128, 128), 128)
        spread_y = product((tall[0, rows], tall[1, rows]), adverse)
        real, imag = blocks(spread_y, 0), -blocks(spread_y, 1)
        four = pl.ds(to * 4, 4)
        ys[four, 0] = jnp.where(first, real, swap_parts(imag)).reshape(4, ROWS, 128)
        ys[four, 1] = jnp.where(first, swap_parts(real), imag).reshape(4, ROWS, 128)
        for k in (2, 1, 3, 0):
            if k != 0 or m != 0:
                backward(to * 4 + (row + k) % 4).start()
    h[pen] = ys[pen]

    step = weight_factor * time_step
    for k in range(1, PEN):
        backward_from((pen + k) % PEN).wait_recv()
    turned_x = [turn([h[4 * q + j].reshape(2 * ROWS, 128) for j in range(4)]) for q in range(4)]
    for level in range(LEVELS):
        chunks = [turned_x[q][level] for q in range(4)]
        gathered_x = jnp.concatenate(
            [jnp.concatenate(chunks, axis=1),
             jnp.concatenate([-sign * swap_parts(chunk) for chunk in chunks], axis=1)], axis=0
        )
        spectra = product(split(gathered_x), table)
        for field in range(2):
            for part in range(2):
                at = slice(GRID * part, GRID * (part + 1))
                start = (2 * part + field) * ROWS
                value = lin[field, level, :, at] - spectra[start : start + ROWS]
                accum_next[field, level, :, at] = value
                state_next[field, level, :, at] = st[field, level, :, at] + step * value

    for k in range(1, groups):
        gather((pair + k) % groups).wait_send()
    for part in range(2):
        swap(part, core).wait_send()
    for k in range(1, PEN):
        forward_from(k).wait_send()
        backward_from((pen + k) % PEN).wait_send()


def on_device(groups, state, accum, base_flow):
    rows_y = GRID // (2 * groups)
    wide, tall = tables()
    fields = (2, LEVELS, ROWS, 2 * GRID)
    result = jax.ShapeDtypeStruct(fields, F32)
    dma = pltpu.SemaphoreType.DMA
    outputs = pl.pallas_call(
        functools.partial(kernel, groups),
        out_shape=(result, result),
        in_specs=[pl.BlockSpec(memory_space=pltpu.HBM)] * 5,
        out_specs=(pl.BlockSpec(memory_space=pltpu.VMEM),) * 2,
        scratch_shapes=[
            pltpu.VMEM(fields, F32),
            pltpu.VMEM(fields, F32),
            pltpu.VMEM((6, LEVELS, rows_y, 16), F32),
            pltpu.VMEM((2, GRID, 2 * GRID), BF16),
            pltpu.VMEM((2, 2 * GRID, GRID), BF16),
            pltpu.VMEM((6 * LEVELS * ROWS, GRID), BF16),
            pltpu.VMEM((6 * LEVELS * ROWS, GRID), BF16),
            pltpu.VMEM((PEN, 3, ROWS, 128), F32),
            pltpu.VMEM((PEN, 3, ROWS, 128), F32),
            pltpu.VMEM((groups, 2, rows_y, 384), F32),
            pltpu.VMEM((PEN, 2, ROWS, 128), F32),
            pltpu.VMEM((PEN, 2, ROWS, 128), F32),
            pltpu.VMEM(fields, F32),
            dma((5,)),
            dma((PEN,)),
            dma((PEN,)),
            dma((PEN,)),
            dma((PEN,)),
            dma((2,)),
            dma((2,)),
            dma((groups,)),
            dma((groups,)),
            dma((1,)),
            pltpu.SemaphoreType.REGULAR((groups,)),
        ],
        compiler_params=pltpu.CompilerParams(
            collective_id=0, has_side_effects=True, vmem_limit_bytes=40 * 1024 * 1024
        ),
        name="step",
    )(*[pltpu.with_memory_space_constraint(x, pltpu.HBM) for x in (
        state.reshape(fields), accum.reshape(fields), base_flow.transpose(0, 1, 3, 2),
        jnp.asarray(wide), jnp.asarray(tall))]
    )
    return tuple(out.reshape(state.shape) for out in outputs)


def solution(mesh):
    spectral = P(None, "ens", None, "pen", None)
    return jax.shard_map(
        functools.partial(on_device, mesh.shape["ens"] // 2),
        mesh=mesh,
        in_specs=(spectral, spectral, P(None, None, "pen", "ens")),
        out_specs=(spectral, spectral),
        check_vma=False,
    )
```

```python
import functools
import math

import jax
import jax.numpy as jnp
import numpy as np
from jax import lax
from jax.experimental import pallas as pl
from jax.experimental.pallas import tpu as pltpu
from jax.sharding import PartitionSpec as P

viscosity = 0.05
vertical_mixing = 0.5
buoyancy_gain = 0.5
stratification = 0.5
memory_factor = -5.0 / 9.0
weight_factor = 15.0 / 16.0
time_step = 0.4

GRID = 256
LEVELS = 4
ROWS = 16
PEN = 16
CHUNK = 16
MESH = pl.DeviceIdType.MESH
F32 = jnp.float32
BF16 = jnp.bfloat16


def halves(table):
    high = table.astype(np.float32).astype(jnp.bfloat16)
    low = (table - high.astype(np.float64)).astype(np.float32).astype(jnp.bfloat16)
    return np.stack([high, low])


def tables():
    position = np.arange(GRID)
    angle = 2.0 * np.pi / GRID * (position[:, None] * position[None, :] % GRID)
    table = np.stack([np.cos(angle), np.sin(angle)], 1).reshape(GRID, 2, GRID // CHUNK, CHUNK)
    table = table.transpose(0, 2, 1, 3).reshape(GRID, 2 * GRID) / 16.0
    return halves(table), halves(table.T.copy())


def split(value):
    high = value.astype(BF16)
    return high, (value - high.astype(F32)).astype(BF16)


def dot(a, b):
    return jnp.dot(a, b, preferred_element_type=F32)


def product(a, b):
    return dot(a[0], b[0]) + (dot(a[1], b[0]) + dot(a[0], b[1]))


def wave_numbers(shape, dim, offset):
    position = lax.broadcasted_iota(jnp.int32, shape, dim) + offset
    signed = jnp.where(position <= GRID // 2, position, position - GRID)
    derivative = jnp.where(position == GRID // 2, 0, signed)
    return (2.0 * math.pi / GRID) * derivative.astype(F32), signed


def kernel(
    groups,
    state_hbm, accum_hbm, base_hbm, wide_hbm, tall_hbm,
    state_next, accum_next,
    st, ac, bs, wide, tall, pk_high, pk_low, xs, g, bb, ys, h, lin,
    load_sem, fs, fr, rs, rr, cs, cr, hs, hr, here,
):
    ens = lax.axis_index("ens")
    pen = lax.axis_index("pen")
    pair, core = ens // 2, ens % 2
    column, row = pen // 4, pen % 4
    other = ens + 1 - 2 * core
    rows_y = GRID // (2 * groups)

    barrier = pltpu.get_barrier_semaphore()
    for k in range(1, PEN):
        pl.semaphore_signal(barrier, inc=1, device_id=(ens, (pen + k) % PEN), device_id_type=MESH)
    pl.semaphore_signal(barrier, inc=1, device_id=(other, pen), device_id_type=MESH)
    for k in range(1, groups):

        @pl.when(pair + k < groups)
        def _():
            pl.semaphore_signal(
                barrier, inc=1, device_id=((pair + k) * 2 + core, pen), device_id_type=MESH
            )

    loads = [
        pltpu.make_async_copy(source, target, load_sem.at[i])
        for i, (source, target) in enumerate(
            [(base_hbm, bs), (state_hbm, st), (wide_hbm, wide), (tall_hbm, tall), (accum_hbm, ac)]
        )
    ]
    for load in loads:
        load.start()

    lane = lax.broadcasted_iota(jnp.int32, (1, 128), 1)
    first = lane // CHUNK % 2 == 0
    sign = jnp.where(first, -1.0, 1.0)

    def swap_parts(value):
        return jnp.where(
            first, pltpu.roll(value, 128 - CHUNK, 1), pltpu.roll(value, CHUNK, 1)
        )

    def turn(values):
        results = []
        for j in range(4):
            result = None
            for l in range(4):
                moved = values[l] if l == j else pltpu.roll(values[l], 32 * (l - j) % 128, 1)
                result = moved if result is None else jnp.where(lane // 32 == l, moved, result)
            results.append(result)
        return results

    half = groups // 2
    quarter = groups // 4
    pl.semaphore_wait(barrier, PEN + pair)
    for k in range(1, groups):

        @pl.when(pair - k >= 0)
        def _():
            pl.semaphore_signal(
                here.at[pair // half],
                inc=1,
                device_id=((pair - k) * 2 + core, pen),
                device_id_type=MESH,
            )

    loads[0].wait()
    place = (
        lax.broadcasted_iota(jnp.int32, (CHUNK, 128), 1) % CHUNK
        == lax.broadcasted_iota(jnp.int32, (CHUNK, 128), 0)
    ).astype(F32)
    placed = lax.dot_general(
        bs[...].reshape(6 * LEVELS * rows_y, CHUNK), place, (((1,), (0,)), ((), ())),
        precision=lax.Precision.HIGHEST, preferred_element_type=F32,
    ).reshape(6, LEVELS, rows_y, 128)
    for q in range(3):
        result = placed[2 * q, 0]
        for group in range(1, 8):
            result = jnp.where(
                lane // CHUNK == group, placed[2 * q + group % 2, group // 2], result
            )
        bb[pair, core, :, 128 * q : 128 * (q + 1)] = result

    def gather(target):
        return pltpu.make_async_remote_copy(
            src_ref=bb.at[pair, core],
            dst_ref=bb.at[pair, core],
            send_sem=hs.at[0],
            recv_sem=hr.at[pair // quarter],
            device_id=(target * 2 + core, pen),
            device_id_type=MESH,
        )

    def pieces(count, sem):
        return pltpu.make_async_remote_copy(
            src_ref=bb.at[:count, 0],
            dst_ref=bb.at[:count, 0],
            send_sem=hs.at[0],
            recv_sem=sem,
            device_id=(other, pen),
            device_id_type=MESH,
        )

    for target in range(groups - 1):

        @pl.when(target < pair)
        def _():
            gather(target).start()

    kappa_y, signed_y = wave_numbers((ROWS, 1), 0, pen * ROWS)
    kappa_x, signed_x = wave_numbers((1, GRID), 1, 0)
    wave_square = signed_y * signed_y + signed_x * signed_x
    factor = (2.0 * math.pi / GRID) ** 2
    square = factor * wave_square.astype(F32)
    inverse = jnp.where(
        wave_square > 0, 1.0 / (factor * jnp.maximum(wave_square, 1).astype(F32)), 0.0
    )

    loads[1].wait()
    loads[2].wait()

    packed = []
    for level in range(LEVELS):
        zr, zi = st[0, level, :, :GRID], st[0, level, :, GRID:]
        tr, ti = st[1, level, :, :GRID], st[1, level, :, GRID:]
        wzr, wzi = kappa_x * zr - kappa_y * zi, kappa_x * zi + kappa_y * zr
        wtr, wti = kappa_x * tr - kappa_y * ti, kappa_x * ti + kappa_y * tr
        packed += [wzr * inverse, -wzi, -wti, wzi * inverse, wzr, wtr]
    pk_high[...], pk_low[...] = split(jnp.concatenate(packed, axis=0))

    def forward(target):
        return pltpu.make_async_remote_copy(
            src_ref=xs.at[target],
            dst_ref=g.at[pen],
            send_sem=fs.at[0],
            recv_sem=fr.at[0],
            device_id=(ens, target),
            device_id_type=MESH,
        )

    for m in (2, 1, 3, 0):
        to = (column + m) % 4
        at = pl.ds(pl.multiple_of(to * 128, 128), 128)
        mixed = product((pk_high[...], pk_low[...]), (wide[0, :, at], wide[1, :, at]))
        mixed = mixed.reshape(LEVELS, 2, 3 * ROWS, 128)
        parts = turn([mixed[l, 0] + sign * swap_parts(mixed[l, 1]) for l in range(LEVELS)])
        for j in range(4):
            xs[to * 4 + j] = parts[j].reshape(3, ROWS, 128)
        for k in (2, 1, 3, 0):
            if k != 0 or m != 0:
                forward(to * 4 + (row + k) % 4).start()
    g[pen] = xs[pen]
    for part in range(2):
        waits = jnp.where(pair // half == part, half * (part + 1) - 1 - pair, half)
        waits = jnp.where(pair // half > part, 0, waits)

        @pl.when(waits > 0)
        def _():
            pl.semaphore_wait(here.at[part], waits)

        for target in range(half * part, half * (part + 1)):

            @pl.when(pair < target)
            def _():
                gather(target).start()

    loads[4].wait()
    for level in range(LEVELS):
        up, down = min(level + 1, LEVELS - 1), max(level - 1, 0)
        zr, zi = st[0, level, :, :GRID], st[0, level, :, GRID:]
        tr, ti = st[1, level, :, :GRID], st[1, level, :, GRID:]
        across = stratification * kappa_x * inverse
        linear = (
            jnp.concatenate([-buoyancy_gain * kappa_x * ti, buoyancy_gain * kappa_x * tr], axis=1),
            jnp.concatenate([-across * zi, across * zr], axis=1),
        )
        damping = viscosity * jnp.concatenate([square, square], axis=1)
        for field in range(2):
            value = st[field, level]
            mixing = st[field, up] + st[field, down] - 2.0 * value
            lin[field, level] = (
                memory_factor * ac[field, level]
                + linear[field]
                - damping * value
                + vertical_mixing * mixing
            )

    def swap(part, side):
        return pltpu.make_async_remote_copy(
            src_ref=bb.at[quarter * part : quarter * (part + 1), side],
            dst_ref=bb.at[quarter * part : quarter * (part + 1), side],
            send_sem=cs.at[0],
            recv_sem=cr.at[0],
            device_id=(other, pen),
            device_id_type=MESH,
        )

    for part in range(4):

        @pl.when(pair // quarter == part)
        def _():
            pieces(quarter - 1, hr.at[part]).wait_recv()

        @pl.when(pair // quarter != part)
        def _():
            pieces(quarter, hr.at[part]).wait_recv()

        swap(part, core).start()

    def others(sent, received, sems):
        return pltpu.make_async_remote_copy(
            src_ref=sent.at[: PEN - 1],
            dst_ref=received.at[: PEN - 1],
            send_sem=sems[0].at[0],
            recv_sem=sems[1].at[0],
            device_id=(other, pen),
            device_id_type=MESH,
        )

    others(xs, g, (fs, fr)).wait_recv()

    loads[3].wait()
    table = (tall[0], tall[1])
    spectral = jnp.concatenate([g[:, f].reshape(GRID, 128) for f in range(3)], axis=1)
    turned = product(table, split(spectral))
    def blocks(value, part):
        rows = value.reshape(value.shape[0] // 32, 2, CHUNK, 128)[:, part]
        return rows.reshape(value.shape[0] // 2, 128)

    physical = []
    for f in range(3):
        one = turned[:, 128 * f : 128 * (f + 1)]
        physical.append(blocks(one, 0) + sign * swap_parts(blocks(one, 1)))

    whole_swap = pltpu.make_async_remote_copy(
        src_ref=bb.at[:, 0],
        dst_ref=bb.at[:, 0],
        send_sem=cs.at[0],
        recv_sem=cr.at[0],
        device_id=(other, pen),
        device_id_type=MESH,
    )
    whole_swap.wait_recv()
    base = bb[...].reshape(GRID, 384)
    flow, vort_slope, buoy_slope = base[:, :128], base[:, 128:256], base[:, 256:]
    advect_vort = flow * physical[1] + vort_slope * physical[0]
    advect_buoy = flow * physical[2] + buoy_slope * physical[0]
    advect = jnp.where(
        first, advect_vort + swap_parts(advect_vort), advect_buoy + swap_parts(advect_buoy)
    )
    adverse = split(advect)

    def backward(target):
        return pltpu.make_async_remote_copy(
            src_ref=ys.at[target],
            dst_ref=h.at[pen],
            send_sem=rs.at[0],
            recv_sem=rr.at[0],
            device_id=(ens, target),
            device_id_type=MESH,
        )

    for m in (2, 1, 3, 0):
        to = (column + m) % 4
        rows = pl.ds(pl.multiple_of(to * 128, 128), 128)
        spread_y = product((tall[0, rows], tall[1, rows]), adverse)
        real, imag = blocks(spread_y, 0), -blocks(spread_y, 1)
        four = pl.ds(to * 4, 4)
        ys[four, 0] = jnp.where(first, real, swap_parts(imag)).reshape(4, ROWS, 128)
        ys[four, 1] = jnp.where(first, swap_parts(real), imag).reshape(4, ROWS, 128)
        for k in (2, 1, 3, 0):
            if k != 0 or m != 0:
                backward(to * 4 + (row + k) % 4).start()
    h[pen] = ys[pen]

    step = weight_factor * time_step
    others(ys, h, (rs, rr)).wait_recv()
    turned_x = [turn([h[4 * q + j].reshape(2 * ROWS, 128) for j in range(4)]) for q in range(4)]
    for level in range(LEVELS):
        chunks = [turned_x[q][level] for q in range(4)]
        gathered_x = jnp.concatenate(
            [jnp.concatenate(chunks, axis=1),
             jnp.concatenate([-sign * swap_parts(chunk) for chunk in chunks], axis=1)], axis=0
        )
        spectra = product(split(gathered_x), table)
        for field in range(2):
            for part in range(2):
                at = slice(GRID * part, GRID * (part + 1))
                start = (2 * part + field) * ROWS
                value = lin[field, level, :, at] - spectra[start : start + ROWS]
                accum_next[field, level, :, at] = value
                state_next[field, level, :, at] = st[field, level, :, at] + step * value

    pieces(groups - 1, hr.at[0]).wait_send()
    whole_swap.wait_send()
    others(xs, g, (fs, fr)).wait_send()
    others(ys, h, (rs, rr)).wait_send()


def on_device(groups, state, accum, base_flow):
    rows_y = GRID // (2 * groups)
    wide, tall = tables()
    fields = (2, LEVELS, ROWS, 2 * GRID)
    result = jax.ShapeDtypeStruct(fields, F32)
    dma = pltpu.SemaphoreType.DMA
    outputs = pl.pallas_call(
        functools.partial(kernel, groups),
        out_shape=(result, result),
        in_specs=[pl.BlockSpec(memory_space=pltpu.HBM)] * 5,
        out_specs=(pl.BlockSpec(memory_space=pltpu.VMEM),) * 2,
        scratch_shapes=[
            pltpu.VMEM(fields, F32),
            pltpu.VMEM(fields, F32),
            pltpu.VMEM((6, LEVELS, rows_y, 16), F32),
            pltpu.VMEM((2, GRID, 2 * GRID), BF16),
            pltpu.VMEM((2, 2 * GRID, GRID), BF16),
            pltpu.VMEM((6 * LEVELS * ROWS, GRID), BF16),
            pltpu.VMEM((6 * LEVELS * ROWS, GRID), BF16),
            pltpu.VMEM((PEN, 3, ROWS, 128), F32),
            pltpu.VMEM((PEN, 3, ROWS, 128), F32),
            pltpu.VMEM((groups, 2, rows_y, 384), F32),
            pltpu.VMEM((PEN, 2, ROWS, 128), F32),
            pltpu.VMEM((PEN, 2, ROWS, 128), F32),
            pltpu.VMEM(fields, F32),
            dma((5,)),
            dma((1,)),
            dma((1,)),
            dma((1,)),
            dma((1,)),
            dma((1,)),
            dma((1,)),
            dma((1,)),
            dma((4,)),
            pltpu.SemaphoreType.REGULAR((2,)),
        ],
        compiler_params=pltpu.CompilerParams(
            collective_id=0, has_side_effects=True, vmem_limit_bytes=40 * 1024 * 1024
        ),
        name="step",
    )(*[pltpu.with_memory_space_constraint(x, pltpu.HBM) for x in (
        state.reshape(fields), accum.reshape(fields), base_flow.transpose(0, 1, 3, 2),
        jnp.asarray(wide), jnp.asarray(tall))]
    )
    return tuple(out.reshape(state.shape) for out in outputs)


def solution(mesh):
    spectral = P(None, "ens", None, "pen", None)
    return jax.shard_map(
        functools.partial(on_device, mesh.shape["ens"] // 2),
        mesh=mesh,
        in_specs=(spectral, spectral, P(None, None, "pen", "ens")),
        out_specs=(spectral, spectral),
        check_vma=False,
    )
```

```python
import functools
import math

import jax
import jax.numpy as jnp
import numpy as np
from jax import lax
from jax.experimental import pallas as pl
from jax.experimental.pallas import tpu as pltpu
from jax.sharding import PartitionSpec as P

viscosity = 0.05
vertical_mixing = 0.5
buoyancy_gain = 0.5
stratification = 0.5
memory_factor = -5.0 / 9.0
weight_factor = 15.0 / 16.0
time_step = 0.4

GRID = 256
LEVELS = 4
ROWS = 16
PEN = 16
CHUNK = 16
MESH = pl.DeviceIdType.MESH
F32 = jnp.float32
BF16 = jnp.bfloat16


def halves(table):
    high = table.astype(np.float32).astype(jnp.bfloat16)
    low = (table - high.astype(np.float64)).astype(np.float32).astype(jnp.bfloat16)
    return np.stack([high, low])


def tables():
    position = np.arange(GRID)
    angle = 2.0 * np.pi / GRID * (position[:, None] * position[None, :] % GRID)
    table = np.stack([np.cos(angle), np.sin(angle)], 1).reshape(GRID, 2, GRID // CHUNK, CHUNK)
    table = table.transpose(0, 2, 1, 3).reshape(GRID, 2 * GRID) / 16.0
    return halves(table), halves(table.T.copy())


def split(value):
    high = value.astype(BF16)
    return high, (value - high.astype(F32)).astype(BF16)


def dot(a, b):
    return jnp.dot(a, b, preferred_element_type=F32)


def product(a, b):
    return dot(a[0], b[0]) + (dot(a[1], b[0]) + dot(a[0], b[1]))


def wave_numbers(shape, dim, offset):
    position = lax.broadcasted_iota(jnp.int32, shape, dim) + offset
    signed = jnp.where(position <= GRID // 2, position, position - GRID)
    derivative = jnp.where(position == GRID // 2, 0, signed)
    return (2.0 * math.pi / GRID) * derivative.astype(F32), signed


def kernel(
    groups,
    state_hbm, accum_hbm, base_hbm, wide_hbm, tall_hbm,
    lin, advected,
    st, ac, bs, wide, tall, pk_high, pk_low, xs, g, bb, ys, h,
    load_sem, fs, fr, rs, rr, cs, cr, hs, hr, here,
):
    ens = lax.axis_index("ens")
    pen = lax.axis_index("pen")
    pair, core = ens // 2, ens % 2
    column, row = pen // 4, pen % 4
    other = ens + 1 - 2 * core
    rows_y = GRID // (2 * groups)

    loads = [
        pltpu.make_async_copy(source, target, load_sem.at[i])
        for i, (source, target) in enumerate(
            [(base_hbm, bs), (state_hbm, st), (wide_hbm, wide), (tall_hbm, tall), (accum_hbm, ac)]
        )
    ]
    for load in loads:
        load.start()

    barrier = pltpu.get_barrier_semaphore()
    for k in range(1, PEN):
        pl.semaphore_signal(barrier, inc=1, device_id=(ens, (pen + k) % PEN), device_id_type=MESH)
    pl.semaphore_signal(barrier, inc=1, device_id=(other, pen), device_id_type=MESH)
    for k in range(1, groups):

        @pl.when(pair + k < groups)
        def _():
            pl.semaphore_signal(
                barrier, inc=1, device_id=((pair + k) * 2 + core, pen), device_id_type=MESH
            )

    lane = lax.broadcasted_iota(jnp.int32, (1, 128), 1)
    first = lane // CHUNK % 2 == 0
    sign = jnp.where(first, -1.0, 1.0)

    def swap_parts(value):
        return jnp.where(
            first, pltpu.roll(value, 128 - CHUNK, 1), pltpu.roll(value, CHUNK, 1)
        )

    def turn(values):
        results = []
        for j in range(4):
            result = None
            for l in range(4):
                moved = values[l] if l == j else pltpu.roll(values[l], 32 * (l - j) % 128, 1)
                result = moved if result is None else jnp.where(lane // 32 == l, moved, result)
            results.append(result)
        return results

    half = groups // 2
    quarter = groups // 4
    pl.semaphore_wait(barrier, PEN + pair)
    loads[0].wait()
    place = (
        lax.broadcasted_iota(jnp.int32, (CHUNK, 128), 1) % CHUNK
        == lax.broadcasted_iota(jnp.int32, (CHUNK, 128), 0)
    ).astype(F32)
    placed = lax.dot_general(
        bs[...].reshape(6 * LEVELS * rows_y, CHUNK), place, (((1,), (0,)), ((), ())),
        precision=lax.Precision.HIGHEST, preferred_element_type=F32,
    ).reshape(6, LEVELS, rows_y, 128)
    for q in range(3):
        result = placed[2 * q, 0]
        for group in range(1, 8):
            result = jnp.where(
                lane // CHUNK == group, placed[2 * q + group % 2, group // 2], result
            )
        bb[pair, core, :, 128 * q : 128 * (q + 1)] = result

    def lanes(piece):
        return slice(256 * piece, 256 + 128 * piece)

    def gather(target, piece):
        arrival = pair // quarter if piece == 0 else 4 + pair // half
        return pltpu.make_async_remote_copy(
            src_ref=bb.at[pair, core, :, lanes(piece)],
            dst_ref=bb.at[pair, core, :, lanes(piece)],
            send_sem=hs.at[0],
            recv_sem=hr.at[arrival],
            device_id=(target * 2 + core, pen),
            device_id_type=MESH,
        )

    def pieces(count, piece, sem):
        return pltpu.make_async_remote_copy(
            src_ref=bb.at[:count, 0, :, lanes(piece)],
            dst_ref=bb.at[:count, 0, :, lanes(piece)],
            send_sem=hs.at[0],
            recv_sem=sem,
            device_id=(other, pen),
            device_id_type=MESH,
        )

    def swap(piece, part, size, side):
        block = bb.at[size * part : size * (part + 1), side, :, lanes(piece)]
        return pltpu.make_async_remote_copy(
            src_ref=block,
            dst_ref=block,
            send_sem=cs.at[0],
            recv_sem=cr.at[piece],
            device_id=(other, pen),
            device_id_type=MESH,
        )

    def collect(piece):
        size = quarter if piece == 0 else half
        for part in range(groups // size):
            arrival = hr.at[4 * piece + part]

            @pl.when(pair // size == part)
            def _():
                pieces(size - 1, piece, arrival).wait_recv()

            @pl.when(pair // size != part)
            def _():
                pieces(size, piece, arrival).wait_recv()

            swap(piece, part, size, core).start()

    for piece in range(2):
        for target in range(groups - 1):

            @pl.when(target < pair)
            def _():
                gather(target, piece).start()

    for k in range(1, groups):

        @pl.when(pair - k >= 0)
        def _():
            pl.semaphore_signal(
                here.at[pair // half],
                inc=1,
                device_id=((pair - k) * 2 + core, pen),
                device_id_type=MESH,
            )

    kappa_y, signed_y = wave_numbers((ROWS, 1), 0, pen * ROWS)
    kappa_x, signed_x = wave_numbers((1, GRID), 1, 0)
    wave_square = signed_y * signed_y + signed_x * signed_x
    factor = (2.0 * math.pi / GRID) ** 2
    square = factor * wave_square.astype(F32)
    inverse = jnp.where(
        wave_square > 0, 1.0 / (factor * jnp.maximum(wave_square, 1).astype(F32)), 0.0
    )

    loads[1].wait()
    loads[2].wait()

    packed = []
    for level in range(LEVELS):
        zr, zi = st[0, level, :, :GRID], st[0, level, :, GRID:]
        tr, ti = st[1, level, :, :GRID], st[1, level, :, GRID:]
        wzr, wzi = kappa_x * zr - kappa_y * zi, kappa_x * zi + kappa_y * zr
        wtr, wti = kappa_x * tr - kappa_y * ti, kappa_x * ti + kappa_y * tr
        packed += [wzr * inverse, -wzi, -wti, wzi * inverse, wzr, wtr]
    pk_high[...], pk_low[...] = split(jnp.concatenate(packed, axis=0))

    def forward(target, piece):
        at = slice(2 * piece, 2 + piece)
        return pltpu.make_async_remote_copy(
            src_ref=xs.at[target, at],
            dst_ref=g.at[pen, at],
            send_sem=fs.at[0],
            recv_sem=fr.at[piece],
            device_id=(ens, target),
            device_id_type=MESH,
        )

    for m in (2, 1, 3, 0):
        to = (column + m) % 4
        at = pl.ds(pl.multiple_of(to * 128, 128), 128)
        mixed = product((pk_high[...], pk_low[...]), (wide[0, :, at], wide[1, :, at]))
        mixed = mixed.reshape(LEVELS, 2, 3 * ROWS, 128)
        parts = turn([mixed[l, 0] + sign * swap_parts(mixed[l, 1]) for l in range(LEVELS)])
        for j in range(4):
            xs[to * 4 + j] = parts[j].reshape(3, ROWS, 128)
        for k in (2, 1, 3, 0):
            if k != 0 or m != 0:
                forward(to * 4 + (row + k) % 4, 0).start()
    for m in (2, 1, 3, 0):
        for k in (2, 1, 3, 0):
            if k != 0 or m != 0:
                forward((column + m) % 4 * 4 + (row + k) % 4, 1).start()
    g[pen] = xs[pen]
    for part in range(2):
        waits = jnp.where(pair // half == part, half * (part + 1) - 1 - pair, half)
        waits = jnp.where(pair // half > part, 0, waits)

        @pl.when(waits > 0)
        def _():
            pl.semaphore_wait(here.at[part], waits)

        for piece in range(2):
            for target in range(half * part, half * (part + 1)):

                @pl.when(pair < target)
                def _():
                    gather(target, piece).start()

    loads[4].wait()
    for level in range(LEVELS):
        up, down = min(level + 1, LEVELS - 1), max(level - 1, 0)
        zr, zi = st[0, level, :, :GRID], st[0, level, :, GRID:]
        tr, ti = st[1, level, :, :GRID], st[1, level, :, GRID:]
        across = stratification * kappa_x * inverse
        linear = (
            jnp.concatenate([-buoyancy_gain * kappa_x * ti, buoyancy_gain * kappa_x * tr], axis=1),
            jnp.concatenate([-across * zi, across * zr], axis=1),
        )
        damping = viscosity * jnp.concatenate([square, square], axis=1)
        for field in range(2):
            value = st[field, level]
            mixing = st[field, up] + st[field, down] - 2.0 * value
            lin[field, 0, level] = (
                memory_factor * ac[field, level]
                + linear[field]
                - damping * value
                + vertical_mixing * mixing
            )

    def others(sent, received, send_sem, recv_sem):
        return pltpu.make_async_remote_copy(
            src_ref=sent.at[: PEN - 1],
            dst_ref=received.at[: PEN - 1],
            send_sem=send_sem.at[0],
            recv_sem=recv_sem,
            device_id=(other, pen),
            device_id_type=MESH,
        )

    def blocks(value, part):
        rows = value.reshape(value.shape[0] // 32, 2, CHUNK, 128)[:, part]
        return rows.reshape(value.shape[0] // 2, 128)

    def turn_y(fields):
        spectral = jnp.concatenate([g[:, f].reshape(GRID, 128) for f in fields], axis=1)
        turned = product((tall[0], tall[1]), split(spectral))
        ones = [turned[:, 128 * i : 128 * (i + 1)] for i in range(len(fields))]
        return [blocks(one, 0) + sign * swap_parts(blocks(one, 1)) for one in ones]

    def base(q):
        return bb[:, :, :, 128 * q : 128 * (q + 1)].reshape(GRID, 128)

    def base_swapped(piece):
        whole = bb.at[:, 0, :, lanes(piece)]
        return pltpu.make_async_remote_copy(
            src_ref=whole,
            dst_ref=whole,
            send_sem=cs.at[0],
            recv_sem=cr.at[piece],
            device_id=(other, pen),
            device_id_type=MESH,
        )

    def backward(target, field):
        return pltpu.make_async_remote_copy(
            src_ref=ys.at[target, field],
            dst_ref=h.at[pen, field],
            send_sem=rs.at[0],
            recv_sem=rr.at[field],
            device_id=(ens, target),
            device_id_type=MESH,
        )

    def send_back(field, terms):
        adverse = split(terms + swap_parts(terms))
        for m in (2, 1, 3, 0):
            to = (column + m) % 4
            rows = pl.ds(pl.multiple_of(to * 128, 128), 128)
            spread_y = product((tall[0, rows], tall[1, rows]), adverse)
            result = jnp.where(first, blocks(spread_y, 0), -blocks(spread_y, 1))
            ys[pl.ds(to * 4, 4), field] = result.reshape(4, ROWS, 128)
            for k in (2, 1, 3, 0):
                if k != 0 or m != 0:
                    backward(to * 4 + (row + k) % 4, field).start()
        h[pen, field] = ys[pen, field]


    def finish(field):
        others(ys.at[:, field], h.at[:, field], rs, rr.at[field]).wait_recv()
        turned_x = [turn([h[4 * q + j, field] for j in range(4)]) for q in range(4)]
        rows = [
            jnp.concatenate([turned_x[q][level] for level in range(LEVELS)], axis=0)
            for q in range(4)
        ]
        gathered_x = jnp.concatenate(
            [jnp.concatenate(rows, axis=1),
             jnp.concatenate([-sign * swap_parts(one) for one in rows], axis=1)], axis=0
        )
        spectra = product(split(gathered_x), (tall[0], tall[1]))
        for level in range(LEVELS):
            for part in range(2):
                at = slice(GRID * part, GRID * (part + 1))
                start = (LEVELS * part + level) * ROWS
                advected[field, 0, level, :, at] = spectra[start : start + ROWS]

    collect(0)
    loads[3].wait()
    others(xs.at[:, 0:2], g.at[:, 0:2], fs, fr.at[0]).wait_recv()
    flow, vort_slopes = turn_y((0, 1))
    base_swapped(0).wait_recv()
    send_back(0, base(0) * vort_slopes + base(1) * flow)
    collect(1)
    others(xs.at[:, 2:3], g.at[:, 2:3], fs, fr.at[1]).wait_recv()
    (buoy_slopes,) = turn_y((2,))
    base_swapped(1).wait_recv()
    send_back(1, base(0) * buoy_slopes + base(2) * flow)
    finish(0)
    finish(1)

    for piece in range(2):
        pieces(groups - 1, piece, hr.at[0]).wait_send()
        base_swapped(piece).wait_send()
    others(xs, g, fs, fr.at[0]).wait_send()
    others(ys, h, rs, rr.at[0]).wait_send()


def on_device(groups, state, accum, base_flow):
    rows_y = GRID // (2 * groups)
    wide, tall = tables()
    fields = (2, LEVELS, ROWS, 2 * GRID)
    result = jax.ShapeDtypeStruct(state.shape, F32)
    dma = pltpu.SemaphoreType.DMA
    linear, advected = pl.pallas_call(
        functools.partial(kernel, groups),
        out_shape=(result, result),
        in_specs=[pl.BlockSpec(memory_space=pltpu.HBM)] * 5,
        out_specs=(pl.BlockSpec(memory_space=pltpu.VMEM),) * 2,
        scratch_shapes=[
            pltpu.VMEM(fields, F32),
            pltpu.VMEM(fields, F32),
            pltpu.VMEM((6, LEVELS, rows_y, 16), F32),
            pltpu.VMEM((2, GRID, 2 * GRID), BF16),
            pltpu.VMEM((2, 2 * GRID, GRID), BF16),
            pltpu.VMEM((6 * LEVELS * ROWS, GRID), BF16),
            pltpu.VMEM((6 * LEVELS * ROWS, GRID), BF16),
            pltpu.VMEM((PEN, 3, ROWS, 128), F32),
            pltpu.VMEM((PEN, 3, ROWS, 128), F32),
            pltpu.VMEM((groups, 2, rows_y, 384), F32),
            pltpu.VMEM((PEN, 2, ROWS, 128), F32),
            pltpu.VMEM((PEN, 2, ROWS, 128), F32),
            dma((5,)),
            dma((1,)),
            dma((2,)),
            dma((1,)),
            dma((2,)),
            dma((1,)),
            dma((2,)),
            dma((1,)),
            dma((6,)),
            pltpu.SemaphoreType.REGULAR((2,)),
        ],
        compiler_params=pltpu.CompilerParams(
            collective_id=0, has_side_effects=True, vmem_limit_bytes=40 * 1024 * 1024
        ),
        name="step",
    )(*[pltpu.with_memory_space_constraint(x, pltpu.HBM) for x in (
        state.reshape(fields), accum.reshape(fields), base_flow.transpose(0, 1, 3, 2),
        jnp.asarray(wide), jnp.asarray(tall))]
    )
    accum_next = linear - advected
    return state + weight_factor * time_step * accum_next, accum_next


def solution(mesh):
    spectral = P(None, "ens", None, "pen", None)
    return jax.shard_map(
        functools.partial(on_device, mesh.shape["ens"] // 2),
        mesh=mesh,
        in_specs=(spectral, spectral, P(None, None, "pen", "ens")),
        out_specs=(spectral, spectral),
        check_vma=False,
    )
```

```python
import functools
import math

import jax
import jax.numpy as jnp
import numpy as np
from jax import lax
from jax.experimental import pallas as pl
from jax.experimental.pallas import tpu as pltpu
from jax.sharding import PartitionSpec as P

viscosity = 0.05
vertical_mixing = 0.5
buoyancy_gain = 0.5
stratification = 0.5
memory_factor = -5.0 / 9.0
weight_factor = 15.0 / 16.0
time_step = 0.4

GRID = 256
LEVELS = 4
ROWS = 16
PEN = 16
CHUNK = 16
MESH = pl.DeviceIdType.MESH
F32 = jnp.float32
BF16 = jnp.bfloat16


def halves(table):
    high = table.astype(np.float32).astype(jnp.bfloat16)
    low = (table - high.astype(np.float64)).astype(np.float32).astype(jnp.bfloat16)
    return np.stack([high, low])


def tables():
    position = np.arange(GRID)
    angle = 2.0 * np.pi / GRID * (position[:, None] * position[None, :] % GRID)
    table = np.stack([np.cos(angle), np.sin(angle)], 1).reshape(GRID, 2, GRID // CHUNK, CHUNK)
    table = table.transpose(0, 2, 1, 3).reshape(GRID, 2 * GRID) / 16.0
    return halves(table), halves(table.T.copy())


def split(value):
    high = value.astype(BF16)
    return high, (value - high.astype(F32)).astype(BF16)


def dot(a, b):
    return jnp.dot(a, b, preferred_element_type=F32)


def product(a, b):
    return dot(a[0], b[0]) + (dot(a[1], b[0]) + dot(a[0], b[1]))


def wave_numbers(shape, dim, offset):
    position = lax.broadcasted_iota(jnp.int32, shape, dim) + offset
    signed = jnp.where(position <= GRID // 2, position, position - GRID)
    derivative = jnp.where(position == GRID // 2, 0, signed)
    return (2.0 * math.pi / GRID) * derivative.astype(F32), signed


def kernel(
    groups,
    state_hbm, accum_hbm, base_hbm, wide_hbm, tall_hbm,
    lin, advected,
    st, ac, bs, wide, tall, pk_high, pk_low, xs, g, bb, ys, h,
    load_sem, fs, fr, rs, rr, cs, cr, hs, hr, here,
):
    ens = lax.axis_index("ens")
    pen = lax.axis_index("pen")
    pair, core = ens // 2, ens % 2
    column, row = pen // 4, pen % 4
    other = ens + 1 - 2 * core
    rows_y = GRID // (2 * groups)

    loads = [
        pltpu.make_async_copy(source, target, load_sem.at[i])
        for i, (source, target) in enumerate(
            [(base_hbm, bs), (state_hbm, st), (wide_hbm, wide), (tall_hbm, tall), (accum_hbm, ac)]
        )
    ]
    for load in loads:
        load.start()

    barrier = pltpu.get_barrier_semaphore()
    for k in range(1, PEN):
        pl.semaphore_signal(barrier, inc=1, device_id=(ens, (pen + k) % PEN), device_id_type=MESH)
    pl.semaphore_signal(barrier, inc=1, device_id=(other, pen), device_id_type=MESH)
    for k in range(1, groups):

        @pl.when(pair + k < groups)
        def _():
            pl.semaphore_signal(
                barrier, inc=1, device_id=((pair + k) * 2 + core, pen), device_id_type=MESH
            )

    lane = lax.broadcasted_iota(jnp.int32, (1, 128), 1)
    first = lane // CHUNK % 2 == 0
    sign = jnp.where(first, -1.0, 1.0)

    def swap_parts(value):
        return jnp.where(
            first, pltpu.roll(value, 128 - CHUNK, 1), pltpu.roll(value, CHUNK, 1)
        )

    def turn(values):
        results = []
        for j in range(4):
            result = None
            for l in range(4):
                moved = values[l] if l == j else pltpu.roll(values[l], 32 * (l - j) % 128, 1)
                result = moved if result is None else jnp.where(lane // 32 == l, moved, result)
            results.append(result)
        return results

    half = groups // 2
    quarter = groups // 4
    pl.semaphore_wait(barrier, PEN + pair)
    for k in range(1, groups):

        @pl.when(pair - k >= 0)
        def _():
            pl.semaphore_signal(
                here.at[pair // half],
                inc=1,
                device_id=((pair - k) * 2 + core, pen),
                device_id_type=MESH,
            )

    loads[0].wait()
    place = (
        lax.broadcasted_iota(jnp.int32, (CHUNK, 128), 1) % CHUNK
        == lax.broadcasted_iota(jnp.int32, (CHUNK, 128), 0)
    ).astype(F32)
    placed = lax.dot_general(
        bs[...].reshape(6 * LEVELS * rows_y, CHUNK), place, (((1,), (0,)), ((), ())),
        precision=lax.Precision.HIGHEST, preferred_element_type=F32,
    ).reshape(6, LEVELS, rows_y, 128)
    for q in range(3):
        result = placed[2 * q, 0]
        for group in range(1, 8):
            result = jnp.where(
                lane // CHUNK == group, placed[2 * q + group % 2, group // 2], result
            )
        bb[pair, core, :, 128 * q : 128 * (q + 1)] = result

    def lanes(piece):
        return slice(256 * piece, 256 + 128 * piece)

    def gather(target, piece):
        arrival = pair // quarter if piece == 0 else 4 + pair // half
        return pltpu.make_async_remote_copy(
            src_ref=bb.at[pair, core, :, lanes(piece)],
            dst_ref=bb.at[pair, core, :, lanes(piece)],
            send_sem=hs.at[0],
            recv_sem=hr.at[arrival],
            device_id=(target * 2 + core, pen),
            device_id_type=MESH,
        )

    def pieces(count, piece, sem):
        return pltpu.make_async_remote_copy(
            src_ref=bb.at[:count, 0, :, lanes(piece)],
            dst_ref=bb.at[:count, 0, :, lanes(piece)],
            send_sem=hs.at[0],
            recv_sem=sem,
            device_id=(other, pen),
            device_id_type=MESH,
        )

    def swap(piece, part, size, side):
        block = bb.at[size * part : size * (part + 1), side, :, lanes(piece)]
        return pltpu.make_async_remote_copy(
            src_ref=block,
            dst_ref=block,
            send_sem=cs.at[0],
            recv_sem=cr.at[piece],
            device_id=(other, pen),
            device_id_type=MESH,
        )

    def collect(piece):
        size = quarter if piece == 0 else half
        for part in range(groups // size):
            arrival = hr.at[4 * piece + part]

            @pl.when(pair // size == part)
            def _():
                pieces(size - 1, piece, arrival).wait_recv()

            @pl.when(pair // size != part)
            def _():
                pieces(size, piece, arrival).wait_recv()

            swap(piece, part, size, core).start()

    for piece in range(2):
        for target in range(groups - 1):

            @pl.when(target < pair)
            def _():
                gather(target, piece).start()

    kappa_y, signed_y = wave_numbers((ROWS, 1), 0, pen * ROWS)
    kappa_x, signed_x = wave_numbers((1, GRID), 1, 0)
    wave_square = signed_y * signed_y + signed_x * signed_x
    factor = (2.0 * math.pi / GRID) ** 2
    square = factor * wave_square.astype(F32)
    inverse = jnp.where(
        wave_square > 0, 1.0 / (factor * jnp.maximum(wave_square, 1).astype(F32)), 0.0
    )

    loads[1].wait()
    loads[2].wait()

    packed = []
    for level in range(LEVELS):
        zr, zi = st[0, level, :, :GRID], st[0, level, :, GRID:]
        tr, ti = st[1, level, :, :GRID], st[1, level, :, GRID:]
        wzr, wzi = kappa_x * zr - kappa_y * zi, kappa_x * zi + kappa_y * zr
        wtr, wti = kappa_x * tr - kappa_y * ti, kappa_x * ti + kappa_y * tr
        packed += [wzr * inverse, -wzi, -wti, wzi * inverse, wzr, wtr]
    pk_high[...], pk_low[...] = split(jnp.concatenate(packed, axis=0))

    def forward(target, piece):
        at = slice(2 * piece, 2 + piece)
        return pltpu.make_async_remote_copy(
            src_ref=xs.at[target, at],
            dst_ref=g.at[pen, at],
            send_sem=fs.at[0],
            recv_sem=fr.at[piece],
            device_id=(ens, target),
            device_id_type=MESH,
        )

    for m in (2, 1, 3, 0):
        to = (column + m) % 4
        at = pl.ds(pl.multiple_of(to * 128, 128), 128)
        mixed = product((pk_high[...], pk_low[...]), (wide[0, :, at], wide[1, :, at]))
        mixed = mixed.reshape(LEVELS, 2, 3 * ROWS, 128)
        parts = turn([mixed[l, 0] + sign * swap_parts(mixed[l, 1]) for l in range(LEVELS)])
        for j in range(4):
            xs[to * 4 + j] = parts[j].reshape(3, ROWS, 128)
        for k in (2, 1, 3, 0):
            if k != 0 or m != 0:
                forward(to * 4 + (row + k) % 4, 0).start()
    for m in (2, 1, 3, 0):
        for k in (2, 1, 3, 0):
            if k != 0 or m != 0:
                forward((column + m) % 4 * 4 + (row + k) % 4, 1).start()
    g[pen] = xs[pen]
    for part in range(2):
        waits = jnp.where(pair // half == part, half * (part + 1) - 1 - pair, half)
        waits = jnp.where(pair // half > part, 0, waits)

        @pl.when(waits > 0)
        def _():
            pl.semaphore_wait(here.at[part], waits)

        for piece in range(2):
            for target in range(half * part, half * (part + 1)):

                @pl.when(pair < target)
                def _():
                    gather(target, piece).start()

    loads[4].wait()
    for level in range(LEVELS):
        up, down = min(level + 1, LEVELS - 1), max(level - 1, 0)
        zr, zi = st[0, level, :, :GRID], st[0, level, :, GRID:]
        tr, ti = st[1, level, :, :GRID], st[1, level, :, GRID:]
        across = stratification * kappa_x * inverse
        linear = (
            jnp.concatenate([-buoyancy_gain * kappa_x * ti, buoyancy_gain * kappa_x * tr], axis=1),
            jnp.concatenate([-across * zi, across * zr], axis=1),
        )
        damping = viscosity * jnp.concatenate([square, square], axis=1)
        for field in range(2):
            value = st[field, level]
            mixing = st[field, up] + st[field, down] - 2.0 * value
            lin[field, 0, level] = (
                memory_factor * ac[field, level]
                + linear[field]
                - damping * value
                + vertical_mixing * mixing
            )

    def others(sent, received, send_sem, recv_sem):
        return pltpu.make_async_remote_copy(
            src_ref=sent.at[: PEN - 1],
            dst_ref=received.at[: PEN - 1],
            send_sem=send_sem.at[0],
            recv_sem=recv_sem,
            device_id=(other, pen),
            device_id_type=MESH,
        )

    def blocks(value, part):
        rows = value.reshape(value.shape[0] // 32, 2, CHUNK, 128)[:, part]
        return rows.reshape(value.shape[0] // 2, 128)

    def turn_y(fields):
        spectral = jnp.concatenate([g[:, f].reshape(GRID, 128) for f in fields], axis=1)
        turned = product((tall[0], tall[1]), split(spectral))
        ones = [turned[:, 128 * i : 128 * (i + 1)] for i in range(len(fields))]
        return [blocks(one, 0) + sign * swap_parts(blocks(one, 1)) for one in ones]

    def base(q):
        return bb[:, :, :, 128 * q : 128 * (q + 1)].reshape(GRID, 128)

    def base_swapped(piece):
        whole = bb.at[:, 0, :, lanes(piece)]
        return pltpu.make_async_remote_copy(
            src_ref=whole,
            dst_ref=whole,
            send_sem=cs.at[0],
            recv_sem=cr.at[piece],
            device_id=(other, pen),
            device_id_type=MESH,
        )

    def backward(target, field):
        return pltpu.make_async_remote_copy(
            src_ref=ys.at[target, field],
            dst_ref=h.at[pen, field],
            send_sem=rs.at[0],
            recv_sem=rr.at[field],
            device_id=(ens, target),
            device_id_type=MESH,
        )

    def send_back(field, terms):
        adverse = split(terms + swap_parts(terms))
        for m in (2, 1, 3, 0):
            to = (column + m) % 4
            rows = pl.ds(pl.multiple_of(to * 128, 128), 128)
            spread_y = product((tall[0, rows], tall[1, rows]), adverse)
            result = jnp.where(first, blocks(spread_y, 0), -blocks(spread_y, 1))
            ys[pl.ds(to * 4, 4), field] = result.reshape(4, ROWS, 128)
            for k in (2, 1, 3, 0):
                if k != 0 or m != 0:
                    backward(to * 4 + (row + k) % 4, field).start()
        h[pen, field] = ys[pen, field]


    def finish(field):
        others(ys.at[:, field], h.at[:, field], rs, rr.at[field]).wait_recv()
        turned_x = [turn([h[4 * q + j, field] for j in range(4)]) for q in range(4)]
        rows = [
            jnp.concatenate([turned_x[q][level] for level in range(LEVELS)], axis=0)
            for q in range(4)
        ]
        gathered_x = jnp.concatenate(
            [jnp.concatenate(rows, axis=1),
             jnp.concatenate([-sign * swap_parts(one) for one in rows], axis=1)], axis=0
        )
        spectra = product(split(gathered_x), (tall[0], tall[1]))
        for level in range(LEVELS):
            for part in range(2):
                at = slice(GRID * part, GRID * (part + 1))
                start = (LEVELS * part + level) * ROWS
                advected[field, 0, level, :, at] = spectra[start : start + ROWS]

    collect(0)
    loads[3].wait()
    others(xs.at[:, 0:2], g.at[:, 0:2], fs, fr.at[0]).wait_recv()
    flow, vort_slopes = turn_y((0, 1))
    base_swapped(0).wait_recv()
    send_back(0, base(0) * vort_slopes + base(1) * flow)
    collect(1)
    others(xs.at[:, 2:3], g.at[:, 2:3], fs, fr.at[1]).wait_recv()
    (buoy_slopes,) = turn_y((2,))
    base_swapped(1).wait_recv()
    send_back(1, base(0) * buoy_slopes + base(2) * flow)
    finish(0)
    finish(1)

    for piece in range(2):
        pieces(groups - 1, piece, hr.at[0]).wait_send()
        base_swapped(piece).wait_send()
    others(xs, g, fs, fr.at[0]).wait_send()
    others(ys, h, rs, rr.at[0]).wait_send()


def on_device(groups, state, accum, base_flow):
    rows_y = GRID // (2 * groups)
    wide, tall = tables()
    fields = (2, LEVELS, ROWS, 2 * GRID)
    result = jax.ShapeDtypeStruct(state.shape, F32)
    dma = pltpu.SemaphoreType.DMA
    linear, advected = pl.pallas_call(
        functools.partial(kernel, groups),
        out_shape=(result, result),
        in_specs=[pl.BlockSpec(memory_space=pltpu.HBM)] * 5,
        out_specs=(pl.BlockSpec(memory_space=pltpu.VMEM),) * 2,
        scratch_shapes=[
            pltpu.VMEM(fields, F32),
            pltpu.VMEM(fields, F32),
            pltpu.VMEM((6, LEVELS, rows_y, 16), F32),
            pltpu.VMEM((2, GRID, 2 * GRID), BF16),
            pltpu.VMEM((2, 2 * GRID, GRID), BF16),
            pltpu.VMEM((6 * LEVELS * ROWS, GRID), BF16),
            pltpu.VMEM((6 * LEVELS * ROWS, GRID), BF16),
            pltpu.VMEM((PEN, 3, ROWS, 128), F32),
            pltpu.VMEM((PEN, 3, ROWS, 128), F32),
            pltpu.VMEM((groups, 2, rows_y, 384), F32),
            pltpu.VMEM((PEN, 2, ROWS, 128), F32),
            pltpu.VMEM((PEN, 2, ROWS, 128), F32),
            dma((5,)),
            dma((1,)),
            dma((2,)),
            dma((1,)),
            dma((2,)),
            dma((1,)),
            dma((2,)),
            dma((1,)),
            dma((6,)),
            pltpu.SemaphoreType.REGULAR((2,)),
        ],
        compiler_params=pltpu.CompilerParams(
            collective_id=0, has_side_effects=True, vmem_limit_bytes=40 * 1024 * 1024
        ),
        name="step",
    )(*[pltpu.with_memory_space_constraint(x, pltpu.HBM) for x in (
        state.reshape(fields), accum.reshape(fields), base_flow.transpose(0, 1, 3, 2),
        jnp.asarray(wide), jnp.asarray(tall))]
    )
    accum_next = linear - advected
    return state + weight_factor * time_step * accum_next, accum_next


def solution(mesh):
    spectral = P(None, "ens", None, "pen", None)
    return jax.shard_map(
        functools.partial(on_device, mesh.shape["ens"] // 2),
        mesh=mesh,
        in_specs=(spectral, spectral, P(None, None, "pen", "ens")),
        out_specs=(spectral, spectral),
        check_vma=False,
    )
```

```python
import functools
import math

import jax
import jax.numpy as jnp
import numpy as np
from jax import lax
from jax.experimental import pallas as pl
from jax.experimental.pallas import tpu as pltpu
from jax.sharding import PartitionSpec as P

viscosity = 0.05
vertical_mixing = 0.5
buoyancy_gain = 0.5
stratification = 0.5
memory_factor = -5.0 / 9.0
weight_factor = 15.0 / 16.0
time_step = 0.4

GRID = 256
LEVELS = 4
ROWS = 16
PEN = 16
CHUNK = 16
MESH = pl.DeviceIdType.MESH
F32 = jnp.float32
BF16 = jnp.bfloat16


def halves(table):
    high = table.astype(np.float32).astype(jnp.bfloat16)
    low = (table - high.astype(np.float64)).astype(np.float32).astype(jnp.bfloat16)
    return np.stack([high, low])


def tables():
    position = np.arange(GRID)
    angle = 2.0 * np.pi / GRID * (position[:, None] * position[None, :] % GRID)
    table = np.stack([np.cos(angle), np.sin(angle)], 1).reshape(GRID, 2, GRID // CHUNK, CHUNK)
    table = table.transpose(0, 2, 1, 3).reshape(GRID, 2 * GRID) / 16.0
    return halves(table), halves(table.T.copy())


def split(value):
    high = value.astype(BF16)
    return high, (value - high.astype(F32)).astype(BF16)


def dot(a, b):
    return jnp.dot(a, b, preferred_element_type=F32)


def product(a, b):
    return dot(a[0], b[0]) + (dot(a[1], b[0]) + dot(a[0], b[1]))


def wave_numbers(shape, dim, offset):
    position = lax.broadcasted_iota(jnp.int32, shape, dim) + offset
    signed = jnp.where(position <= GRID // 2, position, position - GRID)
    derivative = jnp.where(position == GRID // 2, 0, signed)
    return (2.0 * math.pi / GRID) * derivative.astype(F32), signed


def kernel(
    groups,
    state_hbm, accum_hbm, base_hbm, wide_hbm, tall_hbm,
    lin, advected,
    st, ac, bs, wide, tall, pk_high, pk_low, xs, g, bb, ys, h,
    load_sem, fs, fr, rs, rr, cs, cr, hs, hr, here,
):
    ens = lax.axis_index("ens")
    pen = lax.axis_index("pen")
    pair, core = ens // 2, ens % 2
    column, row = pen // 4, pen % 4
    other = ens + 1 - 2 * core
    rows_y = GRID // (2 * groups)

    loads = [
        pltpu.make_async_copy(source, target, load_sem.at[i])
        for i, (source, target) in enumerate(
            [(base_hbm, bs), (state_hbm, st), (wide_hbm, wide), (tall_hbm, tall), (accum_hbm, ac)]
        )
    ]
    for load in loads:
        load.start()

    barrier = pltpu.get_barrier_semaphore()
    for k in range(1, PEN):
        pl.semaphore_signal(barrier, inc=1, device_id=(ens, (pen + k) % PEN), device_id_type=MESH)
    pl.semaphore_signal(barrier, inc=1, device_id=(other, pen), device_id_type=MESH)
    @pl.loop(pair + 1, groups)
    def _(target):
        pl.semaphore_signal(
            barrier, inc=1, device_id=(target * 2 + core, pen), device_id_type=MESH
        )

    lane = lax.broadcasted_iota(jnp.int32, (1, 128), 1)
    first = lane // CHUNK % 2 == 0
    sign = jnp.where(first, -1.0, 1.0)

    def swap_parts(value):
        return jnp.where(
            first, pltpu.roll(value, 128 - CHUNK, 1), pltpu.roll(value, CHUNK, 1)
        )

    def turn(values):
        results = []
        for j in range(4):
            result = None
            for l in range(4):
                moved = values[l] if l == j else pltpu.roll(values[l], 32 * (l - j) % 128, 1)
                result = moved if result is None else jnp.where(lane // 32 == l, moved, result)
            results.append(result)
        return results

    half = groups // 2
    quarter = groups // 4
    pl.semaphore_wait(barrier, PEN + pair)
    @pl.loop(0, pair)
    def _(target):
        pl.semaphore_signal(
            here.at[pair // half], inc=1, device_id=(target * 2 + core, pen), device_id_type=MESH
        )

    loads[0].wait()
    place = (
        lax.broadcasted_iota(jnp.int32, (CHUNK, 128), 1) % CHUNK
        == lax.broadcasted_iota(jnp.int32, (CHUNK, 128), 0)
    ).astype(F32)
    placed = lax.dot_general(
        bs[...].reshape(6 * LEVELS * rows_y, CHUNK), place, (((1,), (0,)), ((), ())),
        precision=lax.Precision.HIGHEST, preferred_element_type=F32,
    ).reshape(6, LEVELS, rows_y, 128)
    for q in range(3):
        result = placed[2 * q, 0]
        for group in range(1, 8):
            result = jnp.where(
                lane // CHUNK == group, placed[2 * q + group % 2, group // 2], result
            )
        bb[pair, core, :, 128 * q : 128 * (q + 1)] = result

    def lanes(piece):
        return slice(256 * piece, 256 + 128 * piece)

    def gather(target, piece):
        arrival = pair // quarter if piece == 0 else 4 + pair // half
        return pltpu.make_async_remote_copy(
            src_ref=bb.at[pair, core, :, lanes(piece)],
            dst_ref=bb.at[pair, core, :, lanes(piece)],
            send_sem=hs.at[0],
            recv_sem=hr.at[arrival],
            device_id=(target * 2 + core, pen),
            device_id_type=MESH,
        )

    def pieces(count, piece, sem):
        return pltpu.make_async_remote_copy(
            src_ref=bb.at[:count, 0, :, lanes(piece)],
            dst_ref=bb.at[:count, 0, :, lanes(piece)],
            send_sem=hs.at[0],
            recv_sem=sem,
            device_id=(other, pen),
            device_id_type=MESH,
        )

    def swap(piece, part, size, side):
        block = bb.at[size * part : size * (part + 1), side, :, lanes(piece)]
        return pltpu.make_async_remote_copy(
            src_ref=block,
            dst_ref=block,
            send_sem=cs.at[0],
            recv_sem=cr.at[piece],
            device_id=(other, pen),
            device_id_type=MESH,
        )

    def collect(piece):
        size = quarter if piece == 0 else half
        for part in range(groups // size):
            arrival = hr.at[4 * piece + part]

            @pl.when(pair // size == part)
            def _():
                pieces(size - 1, piece, arrival).wait_recv()

            @pl.when(pair // size != part)
            def _():
                pieces(size, piece, arrival).wait_recv()

            swap(piece, part, size, core).start()

    for piece in range(2):
        @pl.loop(0, pair)
        def _(target):
            gather(target, piece).start()

    kappa_y, signed_y = wave_numbers((ROWS, 1), 0, pen * ROWS)
    kappa_x, signed_x = wave_numbers((1, GRID), 1, 0)
    wave_square = signed_y * signed_y + signed_x * signed_x
    factor = (2.0 * math.pi / GRID) ** 2
    square = factor * wave_square.astype(F32)
    inverse = jnp.where(
        wave_square > 0, 1.0 / (factor * jnp.maximum(wave_square, 1).astype(F32)), 0.0
    )

    loads[1].wait()
    loads[2].wait()

    packed = []
    for level in range(LEVELS):
        zr, zi = st[0, level, :, :GRID], st[0, level, :, GRID:]
        tr, ti = st[1, level, :, :GRID], st[1, level, :, GRID:]
        wzr, wzi = kappa_x * zr - kappa_y * zi, kappa_x * zi + kappa_y * zr
        wtr, wti = kappa_x * tr - kappa_y * ti, kappa_x * ti + kappa_y * tr
        packed += [wzr * inverse, -wzi, -wti, wzi * inverse, wzr, wtr]
    pk_high[...], pk_low[...] = split(jnp.concatenate(packed, axis=0))

    def forward(target, piece):
        at = slice(2 * piece, 2 + piece)
        return pltpu.make_async_remote_copy(
            src_ref=xs.at[target, at],
            dst_ref=g.at[pen, at],
            send_sem=fs.at[0],
            recv_sem=fr.at[piece],
            device_id=(ens, target),
            device_id_type=MESH,
        )

    for m in (2, 1, 3, 0):
        to = (column + m) % 4
        at = pl.ds(pl.multiple_of(to * 128, 128), 128)
        mixed = product((pk_high[...], pk_low[...]), (wide[0, :, at], wide[1, :, at]))
        mixed = mixed.reshape(LEVELS, 2, 3 * ROWS, 128)
        parts = turn([mixed[l, 0] + sign * swap_parts(mixed[l, 1]) for l in range(LEVELS)])
        for j in range(4):
            xs[to * 4 + j] = parts[j].reshape(3, ROWS, 128)
        for k in (2, 1, 3, 0):
            if k != 0 or m != 0:
                forward(to * 4 + (row + k) % 4, 0).start()
    for m in (2, 1, 3, 0):
        for k in (2, 1, 3, 0):
            if k != 0 or m != 0:
                forward((column + m) % 4 * 4 + (row + k) % 4, 1).start()
    g[pen] = xs[pen]
    for part in range(2):
        waits = jnp.where(pair // half == part, half * (part + 1) - 1 - pair, half)
        waits = jnp.where(pair // half > part, 0, waits)

        @pl.when(waits > 0)
        def _():
            pl.semaphore_wait(here.at[part], waits)

        for piece in range(2):
            for target in range(half * part, half * (part + 1)):

                @pl.when(pair < target)
                def _():
                    gather(target, piece).start()

    loads[4].wait()
    for level in range(LEVELS):
        up, down = min(level + 1, LEVELS - 1), max(level - 1, 0)
        zr, zi = st[0, level, :, :GRID], st[0, level, :, GRID:]
        tr, ti = st[1, level, :, :GRID], st[1, level, :, GRID:]
        across = stratification * kappa_x * inverse
        linear = (
            jnp.concatenate([-buoyancy_gain * kappa_x * ti, buoyancy_gain * kappa_x * tr], axis=1),
            jnp.concatenate([-across * zi, across * zr], axis=1),
        )
        damping = viscosity * jnp.concatenate([square, square], axis=1)
        for field in range(2):
            value = st[field, level]
            mixing = st[field, up] + st[field, down] - 2.0 * value
            lin[field, 0, level] = (
                memory_factor * ac[field, level]
                + linear[field]
                - damping * value
                + vertical_mixing * mixing
            )

    def others(sent, received, send_sem, recv_sem):
        return pltpu.make_async_remote_copy(
            src_ref=sent.at[: PEN - 1],
            dst_ref=received.at[: PEN - 1],
            send_sem=send_sem.at[0],
            recv_sem=recv_sem,
            device_id=(other, pen),
            device_id_type=MESH,
        )

    def blocks(value, part):
        rows = value.reshape(value.shape[0] // 32, 2, CHUNK, 128)[:, part]
        return rows.reshape(value.shape[0] // 2, 128)

    def turn_y(fields):
        spectral = jnp.concatenate([g[:, f].reshape(GRID, 128) for f in fields], axis=1)
        turned = product((tall[0], tall[1]), split(spectral))
        ones = [turned[:, 128 * i : 128 * (i + 1)] for i in range(len(fields))]
        return [blocks(one, 0) + sign * swap_parts(blocks(one, 1)) for one in ones]

    def base(q):
        return bb[:, :, :, 128 * q : 128 * (q + 1)].reshape(GRID, 128)

    def base_swapped(piece):
        whole = bb.at[:, 0, :, lanes(piece)]
        return pltpu.make_async_remote_copy(
            src_ref=whole,
            dst_ref=whole,
            send_sem=cs.at[0],
            recv_sem=cr.at[piece],
            device_id=(other, pen),
            device_id_type=MESH,
        )

    def backward(target, field):
        return pltpu.make_async_remote_copy(
            src_ref=ys.at[target, field],
            dst_ref=h.at[pen, field],
            send_sem=rs.at[0],
            recv_sem=rr.at[field],
            device_id=(ens, target),
            device_id_type=MESH,
        )

    def send_back(field, terms):
        adverse = split(terms + swap_parts(terms))
        for m in (2, 1, 3, 0):
            to = (column + m) % 4
            rows = pl.ds(pl.multiple_of(to * 128, 128), 128)
            spread_y = product((tall[0, rows], tall[1, rows]), adverse)
            result = jnp.where(first, blocks(spread_y, 0), -blocks(spread_y, 1))
            ys[pl.ds(to * 4, 4), field] = result.reshape(4, ROWS, 128)
            for k in (2, 1, 3, 0):
                if k != 0 or m != 0:
                    backward(to * 4 + (row + k) % 4, field).start()
        h[pen, field] = ys[pen, field]


    def finish(field):
        others(ys.at[:, field], h.at[:, field], rs, rr.at[field]).wait_recv()
        turned_x = [turn([h[4 * q + j, field] for j in range(4)]) for q in range(4)]
        rows = [
            jnp.concatenate([turned_x[q][level] for level in range(LEVELS)], axis=0)
            for q in range(4)
        ]
        gathered_x = jnp.concatenate(
            [jnp.concatenate(rows, axis=1),
             jnp.concatenate([-sign * swap_parts(one) for one in rows], axis=1)], axis=0
        )
        spectra = product(split(gathered_x), (tall[0], tall[1]))
        for level in range(LEVELS):
            for part in range(2):
                at = slice(GRID * part, GRID * (part + 1))
                start = (LEVELS * part + level) * ROWS
                advected[field, 0, level, :, at] = spectra[start : start + ROWS]

    collect(0)
    loads[3].wait()
    others(xs.at[:, 0:2], g.at[:, 0:2], fs, fr.at[0]).wait_recv()
    flow, vort_slopes = turn_y((0, 1))
    base_swapped(0).wait_recv()
    send_back(0, base(0) * vort_slopes + base(1) * flow)
    collect(1)
    others(xs.at[:, 2:3], g.at[:, 2:3], fs, fr.at[1]).wait_recv()
    (buoy_slopes,) = turn_y((2,))
    base_swapped(1).wait_recv()
    send_back(1, base(0) * buoy_slopes + base(2) * flow)
    finish(0)
    finish(1)

    for piece in range(2):
        pieces(groups - 1, piece, hr.at[0]).wait_send()
        base_swapped(piece).wait_send()
    others(xs, g, fs, fr.at[0]).wait_send()
    others(ys, h, rs, rr.at[0]).wait_send()


def on_device(groups, state, accum, base_flow):
    rows_y = GRID // (2 * groups)
    wide, tall = tables()
    fields = (2, LEVELS, ROWS, 2 * GRID)
    result = jax.ShapeDtypeStruct(state.shape, F32)
    dma = pltpu.SemaphoreType.DMA
    linear, advected = pl.pallas_call(
        functools.partial(kernel, groups),
        out_shape=(result, result),
        in_specs=[pl.BlockSpec(memory_space=pltpu.HBM)] * 5,
        out_specs=(pl.BlockSpec(memory_space=pltpu.VMEM),) * 2,
        scratch_shapes=[
            pltpu.VMEM(fields, F32),
            pltpu.VMEM(fields, F32),
            pltpu.VMEM((6, LEVELS, rows_y, 16), F32),
            pltpu.VMEM((2, GRID, 2 * GRID), BF16),
            pltpu.VMEM((2, 2 * GRID, GRID), BF16),
            pltpu.VMEM((6 * LEVELS * ROWS, GRID), BF16),
            pltpu.VMEM((6 * LEVELS * ROWS, GRID), BF16),
            pltpu.VMEM((PEN, 3, ROWS, 128), F32),
            pltpu.VMEM((PEN, 3, ROWS, 128), F32),
            pltpu.VMEM((groups, 2, rows_y, 384), F32),
            pltpu.VMEM((PEN, 2, ROWS, 128), F32),
            pltpu.VMEM((PEN, 2, ROWS, 128), F32),
            dma((5,)),
            dma((1,)),
            dma((2,)),
            dma((1,)),
            dma((2,)),
            dma((1,)),
            dma((2,)),
            dma((1,)),
            dma((6,)),
            pltpu.SemaphoreType.REGULAR((2,)),
        ],
        compiler_params=pltpu.CompilerParams(
            collective_id=0, has_side_effects=True, vmem_limit_bytes=40 * 1024 * 1024
        ),
        name="step",
    )(*[pltpu.with_memory_space_constraint(x, pltpu.HBM) for x in (
        state.reshape(fields), accum.reshape(fields), base_flow.transpose(0, 1, 3, 2),
        jnp.asarray(wide), jnp.asarray(tall))]
    )
    accum_next = linear - advected
    return state + weight_factor * time_step * accum_next, accum_next


def solution(mesh):
    spectral = P(None, "ens", None, "pen", None)
    return jax.shard_map(
        functools.partial(on_device, mesh.shape["ens"] // 2),
        mesh=mesh,
        in_specs=(spectral, spectral, P(None, None, "pen", "ens")),
        out_specs=(spectral, spectral),
        check_vma=False,
    )
```
